256 devices in a mesh: ctx: 64 (over y, z, core), head: 4 (over x).
Axes of the slice: x: 4, y: 4, z: 8, core: 2. Of those that a mesh axis runs over, the one named last changes fastest.
Arguments:
- tokens: bfloat16 [32768, 1024], P(('ctx', 'head')), may hold values from -6 to 6
- conv_kernel: float32 [7, 1024], replicated, may hold values from -2.5 to 2.5
- w_qkv: bfloat16 [1024, 3072], replicated, may hold values from -0.1875 to 0.1875
- w_out: bfloat16 [1024, 1024], replicated, may hold values from -0.1875 to 0.1875
- lengths: int32 [32], replicated, may hold values from 1 to 2048, 32768 in all
- cotangent: bfloat16 [32768, 1024], P(('ctx', 'head')), may hold values from -6 to 6
Outputs:
- attended: bfloat16 [32768, 1024], P(('ctx', 'head'))
- input_grad: bfloat16 [32768, 1024], P(('ctx', 'head'))
The draws below stay inside these ranges and needn't reach their ends.
Inputs may be any that keep to these rules, and one draw needn't show every extreme that they name: `lengths`: they sum to 32768; the longest recording has exactly 2048 tokens.
All inputs are finite; a program needn't handle non-finite values.
Results may differ from the reference program's by a relative error of at most 0.017.
The reference program's roundings to bfloat16 on the way count: a program that leaves them out, or rounds other values in their place, can miss the bound.
Values may be sent and summed in bfloat16 or wider, within the bound.
A program may use at most 128 MiB of HBM per device.

```python
import math
import jax
import jax.numpy as jnp
import numpy as np
from jax import lax

D = 1024
HEADS = 16
HD = 64
KS = 7
MAXLEN = 2048
T_CTX = 512
TOKENS = 32768
NREC = 32


def shard_levels(rng, dims, split, smallest, top_value):
    factor_of, own = 1.0, jax.random.fold_in(rng, 6)
    for axis_at, parts in split:
        draws = jnp.exp(jax.random.uniform(jax.random.fold_in(own, axis_at), (parts,), jnp.float32, smallest / len(split), top_value / len(split)))
        factor_of = factor_of * jnp.repeat(draws, dims[axis_at] // parts).reshape([-1 if axis == axis_at else 1 for axis in range(len(dims))])
    return factor_of


def profile(amount, total, reach, slope):
    weights = [(1 << 20) // math.isqrt(rank ** slope) + 1 for rank in range(2, amount + 1)]
    surplus, counts = total - reach - (amount - 1), [1] * (amount - 1)
    while surplus > 0:
        movable = [i for i in range(amount - 1) if counts[i] < reach]
        whole, remaining = sum([weights[i] for i in movable]), surplus
        for i in movable:
            addition = min(reach - counts[i], max(1, remaining * weights[i] // whole), surplus)
            counts[i] = counts[i] + addition
            surplus = surplus - addition
    return np.array([reach] + counts)


def uneven_parts(stream_key, amount, total, limit, lean):
    if amount == 2:
        one = jax.random.randint(stream_key, (), max(1, total - limit), min(limit, total - 1) + 1)
        return jnp.stack([one, total - one])
    tallies = jnp.asarray(profile(amount, total, limit, lean), jnp.int32)
    couples = (amount - 1) // 2
    donor, taker = tallies[1:1 + 2 * couples:2], tallies[2:2 + 2 * couples:2]
    room = jnp.minimum(donor - 1, limit - taker)
    passed = jax.random.randint(jax.random.fold_in(stream_key, 1), (couples,), 0, 1 << 20) % (room + 1)
    tallies = tallies.at[1:1 + 2 * couples:2].set(donor - passed).at[2:2 + 2 * couples:2].set(taker + passed)
    return tallies[jax.random.permutation(jax.random.fold_in(stream_key, 2), amount)]


def centred(rng, extent, width, most, shards=(), kind=jnp.bfloat16):
    array = jax.random.normal(rng, extent, jnp.float32) * width
    if len(shards) > 0:
        array = shard_levels(rng, extent, shards, -0.22, 0.18) * array
    return jnp.clip(array, min=-most, max=most).astype(kind)


def setup_inputs(seed: int = 0) -> dict:
    arg_keys = jax.random.split(jax.random.key(seed), 7)
    tokens = centred(arg_keys[0], (TOKENS, D), 1.0, 6.0, ((0, 256),))
    conv_kernel = centred(arg_keys[1], (KS, D), 0.3, 2.5, (), jnp.float32)
    w_qkv = centred(arg_keys[2], (D, 3 * D), D ** -0.5, 0.1875)
    w_out = centred(arg_keys[3], (D, D), D ** -0.5, 0.1875)
    lengths = uneven_parts(arg_keys[4], NREC, TOKENS, MAXLEN, 1).astype(jnp.int32)
    cotangent = centred(arg_keys[5], (TOKENS, D), 1.0, 6.0, ((0, 256),))
    return {"tokens": tokens, "conv_kernel": conv_kernel, "w_qkv": w_qkv, "w_out": w_out, "lengths": lengths, "cotangent": cotangent}


def segment_of(positions, lengths):
    record_ends = jnp.cumsum(lengths).astype(jnp.int32)
    return jnp.sum((record_ends[None, :] <= positions[:, None]).astype(jnp.int32), axis=1).astype(jnp.int32)


def convolve(values, kernel, segments):
    count = values.shape[0]
    half_width = KS // 2
    padded = jnp.pad(values.astype(jnp.float32), ((half_width, half_width), (0, 0)))
    seg_padded = jnp.pad(segments, (half_width, half_width), constant_values=-1)
    summed = values.astype(jnp.float32)
    for tap_index in range(KS):
        same_seg = (seg_padded[tap_index:tap_index + count] == segments).astype(jnp.float32)
        summed = summed + kernel[tap_index][None, :] * padded[tap_index:tap_index + count] * same_seg[:, None]
    return summed.astype(jnp.bfloat16)


def rounded(values):
    return lax.optimization_barrier(values.astype(jnp.bfloat16)).astype(jnp.float32)


def reference(tokens, conv_kernel, w_qkv, w_out, lengths, cotangent):
    positions = jnp.arange(TOKENS, dtype=jnp.int32)
    segments = segment_of(positions, lengths)
    mixed = convolve(tokens, conv_kernel, segments)
    projected = jnp.dot(mixed, w_qkv, preferred_element_type=jnp.float32).astype(jnp.bfloat16)
    queries = projected[:, :D].reshape(TOKENS, HEADS, HD)
    key_all = projected[:, D:2 * D].reshape(TOKENS, HEADS, HD)
    value_all = projected[:, 2 * D:].reshape(TOKENS, HEADS, HD)
    score_scale = HD ** -0.5
    blocks = TOKENS // T_CTX
    window = MAXLEN + T_CTX
    key_pad = jnp.pad(key_all, ((MAXLEN, 0), (0, 0), (0, 0)))
    value_pad = jnp.pad(value_all, ((MAXLEN, 0), (0, 0), (0, 0)))
    seg_keys = jnp.pad(segments, (MAXLEN, 0), constant_values=-1)

    def weights_of(block_index):
        first_row = (block_index * T_CTX).astype(jnp.int32)
        query_block = lax.dynamic_slice_in_dim(queries, first_row, T_CTX, 0).astype(jnp.float32)
        key_window = lax.dynamic_slice_in_dim(key_pad, first_row, window, 0).astype(jnp.float32)
        value_window = lax.dynamic_slice_in_dim(value_pad, first_row, window, 0).astype(jnp.float32)
        query_pos = first_row + jnp.arange(T_CTX, dtype=jnp.int32)
        key_pos = first_row - MAXLEN + jnp.arange(window, dtype=jnp.int32)
        seg_query = lax.dynamic_slice_in_dim(segments, first_row, T_CTX, 0)
        seg_key = lax.dynamic_slice_in_dim(seg_keys, first_row, window, 0)
        allowed = (seg_query[:, None] == seg_key[None, :]) & (key_pos[None, :] <= query_pos[:, None])
        scores = jnp.einsum("qhd,khd->hqk", query_block, key_window) * score_scale
        weights = jnp.where(allowed[None], jnp.exp(scores), 0.0)
        return weights, query_block, key_window, value_window, first_row

    def forward_block(block_index):
        weights, query_block, key_window, value_window, first_row = weights_of(block_index)
        totals = jnp.sum(weights, axis=2)
        weighted = jnp.einsum("hqk,khd->qhd", rounded(weights), value_window)
        context = (weighted / totals.T[:, :, None]).astype(jnp.bfloat16)
        return context, totals

    contexts, totals_all = lax.map(forward_block, jnp.arange(blocks, dtype=jnp.int32))
    context_flat = contexts.reshape(TOKENS, D)
    attended = jnp.dot(context_flat, w_out, preferred_element_type=jnp.float32).astype(jnp.bfloat16)
    d_context = jnp.dot(cotangent, w_out.T, preferred_element_type=jnp.float32).astype(jnp.bfloat16)
    d_heads = d_context.reshape(TOKENS, HEADS, HD)
    row_delta = jnp.sum(d_heads.astype(jnp.float32) * contexts.reshape(TOKENS, HEADS, HD).astype(jnp.float32), axis=2)

    def backward_block(carry, block_index):
        d_key_pad, d_value_pad = carry
        weights, query_block, key_window, value_window, first_row = weights_of(block_index)
        totals = totals_all[block_index]
        prob_full = weights / totals[:, :, None]
        d_block = lax.dynamic_slice_in_dim(d_heads, first_row, T_CTX, 0).astype(jnp.float32)
        delta_block = lax.dynamic_slice_in_dim(row_delta, first_row, T_CTX, 0)
        d_values = jnp.einsum("hqk,qhd->khd", rounded(prob_full), d_block)
        d_probs = jnp.einsum("qhd,khd->hqk", d_block, value_window)
        d_scores = rounded(prob_full * (d_probs - delta_block.T[:, :, None]))
        d_query = jnp.einsum("hqk,khd->qhd", d_scores, key_window) * score_scale
        d_keys = jnp.einsum("hqk,qhd->khd", d_scores, query_block) * score_scale
        old_keys = lax.dynamic_slice_in_dim(d_key_pad, first_row, window, 0)
        old_values = lax.dynamic_slice_in_dim(d_value_pad, first_row, window, 0)
        d_key_pad = lax.dynamic_update_slice_in_dim(d_key_pad, old_keys + d_keys, first_row, 0)
        d_value_pad = lax.dynamic_update_slice_in_dim(d_value_pad, old_values + d_values, first_row, 0)
        return (d_key_pad, d_value_pad), d_query

    zeros_pad = jnp.zeros((MAXLEN + TOKENS, HEADS, HD), jnp.float32)
    (d_key_pad, d_value_pad), d_queries = lax.scan(backward_block, (zeros_pad, zeros_pad), jnp.arange(blocks, dtype=jnp.int32))
    grad_q = d_queries.reshape(TOKENS, D).astype(jnp.bfloat16)
    grad_k = d_key_pad[MAXLEN:].reshape(TOKENS, D).astype(jnp.bfloat16)
    grad_v = d_value_pad[MAXLEN:].reshape(TOKENS, D).astype(jnp.bfloat16)
    grad_qkv = jnp.concatenate([grad_q, grad_k, grad_v], axis=1)
    grad_mixed = jnp.dot(grad_qkv, w_qkv.T, preferred_element_type=jnp.float32).astype(jnp.bfloat16)
    input_grad = convolve(grad_mixed, conv_kernel[::-1], segments)
    return attended, input_grad
```

```python
import functools
import math

import jax
import jax.numpy as jnp
from jax import lax
from jax.experimental import pallas as pl
from jax.experimental.pallas import tpu as pltpu
from jax.sharding import PartitionSpec as P

HD = 64
KS = 7
HALO = 16
OWN, PREV, PREVX, PAIR = 0, 1, 2, 3
MESH = pl.DeviceIdType.MESH
F32, BF16, I32 = jnp.float32, jnp.bfloat16, jnp.int32


def nt(a, b):
    return lax.dot_general(a, b, (((1,), (1,)), ((), ())), preferred_element_type=F32)


def nn(a, b):
    return jnp.dot(a, b, preferred_element_type=F32)


def layer_kernel(
    n_ctx,
    tok_hbm,
    cot_hbm,
    wqkv_hbm,
    wout_hbm,
    convk,
    lens,
    att_out,
    ig_out,
    ext,
    ext32,
    cmask,
    cot,
    w3,
    wout,
    mixed,
    kvs,
    qs,
    ds_,
    kv,
    q,
    do,
    kt,
    vt,
    qm,
    dm,
    starts,
    e_ref,
    ot,
    tot,
    of_s,
    of_r,
    tf_s,
    tf_r,
    stat,
    st_s,
    ctxt,
    cxs,
    cx,
    dkv,
    dqt,
    pp_s,
    pp_r,
    sp_s,
    sp_r,
    ps_s,
    ps_r,
    dqf_s,
    dqf_r,
    gs,
    g,
    gm,
    ld,
    s_h,
    r_h,
    s_kv,
    r_kv,
    s_z,
    r_z,
    s_sp,
    r_sp,
    s_pp,
    r_pp,
    s_q,
    r_q,
    s_d,
    r_d,
    s_f,
    r_f,
    s_cx,
    r_cx,
    s_gr,
    r_gr,
    s_g,
    r_g,
):
    c, x = lax.axis_index("ctx"), lax.axis_index("head")
    core = lax.rem(c, 2)
    ahead = lax.rem(c + 2, n_ctx)
    behind = lax.rem(c + n_ctx - 2, n_ctx)
    pair = c + 1 - 2 * core
    rows, width = 128, 256
    seq = 512
    nx = 4
    model = 1024

    up_x = lax.rem(x + 1, nx)
    up_c = lax.rem(c + (x + 1) // nx, n_ctx)
    dn_x = lax.rem(x + nx - 1, nx)
    dn_c = lax.rem(c + n_ctx - (nx - x) // nx, n_ctx)

    loads = [
        pltpu.make_async_copy(tok_hbm, ext.at[pl.ds(HALO, rows), :], ld.at[0]),
        pltpu.make_async_copy(cot_hbm, cot, ld.at[1]),
        pltpu.make_async_copy(wout_hbm, wout, ld.at[2]),
        pltpu.make_async_copy(wqkv_hbm.at[:, pl.ds(model, model)], w3.at[1], ld.at[3]),
        pltpu.make_async_copy(wqkv_hbm.at[:, pl.ds(2 * model, model)], w3.at[2], ld.at[4]),
        pltpu.make_async_copy(wqkv_hbm.at[:, pl.ds(0, model)], w3.at[0], ld.at[5]),
    ]
    for i in (0, 3, 4, 5, 1, 2):
        loads[i].start()

    barrier = pltpu.get_barrier_semaphore()
    peers = [(c, lax.rem(x + d, nx)) for d in (1, 2, 3)]
    peers += [(ahead, x), (behind, x), (pair, x), (up_c, up_x), (dn_c, dn_x)]
    for peer in peers:
        pl.semaphore_signal(barrier, inc=1, device_id=peer, device_id_type=MESH)
    pl.semaphore_wait(barrier, len(peers))

    def send(src, dst, ss, rs, peer):
        copy = pltpu.make_async_remote_copy(
            src_ref=src, dst_ref=dst, send_sem=ss, recv_sem=rs, device_id=peer, device_id_type=MESH
        )
        copy.start()
        return copy

    pending = []

    loads[0].wait()
    h_up = send(ext.at[pl.ds(rows, HALO), :], ext.at[pl.ds(0, HALO), :], s_h.at[0], r_h.at[0], (up_c, up_x))
    h_dn = send(
        ext.at[pl.ds(HALO, HALO), :], ext.at[pl.ds(HALO + rows, HALO), :], s_h.at[1], r_h.at[1], (dn_c, dn_x)
    )

    ends = []
    run = jnp.int32(0)
    for i in range(lens.shape[0]):
        run = run + lens[i]
        ends.append(run)
    lane = lax.broadcasted_iota(I32, (8, seq), 1)
    for qi, shard in ((0, c), (1, ahead)):
        pos = shard * seq + lane
        first = jnp.zeros((8, seq), I32)
        for end in ends:
            first = jnp.where(pos >= end, end, first)
        starts[qi] = first
    row_pos = (c * nx + x) * rows + lax.broadcasted_iota(I32, (rows, 128), 0)
    first = jnp.zeros((rows, 128), I32)
    for end in ends:
        first = jnp.where(row_pos >= end, end, first)
    last = jnp.zeros((rows, 128), I32)
    for end in reversed(ends):
        last = jnp.where(row_pos < end, end, last)
    for t in range(KS):
        near = row_pos + (t - KS // 2)
        cmask[t] = jnp.where((near >= first) & (near < last), 1.0, 0.0).astype(F32)

    def convolve(out, flip):
        def chunk(i, carry):
            lanes = pl.ds(pl.multiple_of(i * 128, 128), 128)
            acc = ext32[pl.ds(HALO, rows), lanes]
            for t in range(KS):
                tap = convk[pl.ds(KS - 1 - t if flip else t, 1), lanes]
                acc = acc + tap * ext32[pl.ds(HALO - KS // 2 + t, rows), lanes] * cmask[t]
            out[:, lanes] = acc.astype(BF16)
            return carry

        lax.fori_loop(0, model // 128, chunk, 0)

    h_up.wait()
    h_dn.wait()
    ext32[...] = ext[...].astype(F32)
    convolve(mixed, False)

    loads[3].wait()
    loads[4].wait()
    kv_sends = []
    for d in (2, 1, 3, 0):
        p = lax.rem(x + d, nx)
        cols = pl.ds(pl.multiple_of(p * width, width), width)
        for part in (0, 1):
            block = nn(mixed[...], w3[1 + part, :, cols]).astype(BF16)
            kvs[d, :, part * width : (part + 1) * width] = block
        if d:
            kv_sends.append(
                (d, send(kvs.at[d], kv.at[OWN, pl.ds(pl.multiple_of(x * rows, rows), rows), :], s_kv.at[d], r_kv.at[d], (c, p)))
            )
        else:
            kv[OWN, pl.ds(pl.multiple_of(x * rows, rows), rows), :] = kvs[0]

    def piece(d):
        return pl.ds(pl.multiple_of(lax.rem(x + nx - d, nx) * rows, rows), rows)

    z_sends, sp_sends = {}, {}

    def forward(d):
        at = piece(d)
        z_sends[d] = send(kv.at[OWN, at, :], kv.at[PREV, at, :], s_z.at[d], r_z.at[d], (ahead, x))
        sp_sends[d] = send(kv.at[OWN, at, :], kv.at[PAIR, at, :], s_sp.at[d], r_sp.at[d], (pair, x))

    forward(0)

    loads[5].wait()
    q_sends = []
    for d in (2, 1, 3, 0):
        p = lax.rem(x + d, nx)
        cols = pl.ds(pl.multiple_of(p * width, width), width)
        block = nn(mixed[...], w3[0, :, cols]).astype(BF16)
        if d:
            qs[d] = block
            q_sends.append(
                send(qs.at[d], q.at[0, pl.ds(pl.multiple_of(x * rows, rows), rows), :], s_q.at[d], r_q.at[d], (c, p))
            )
        else:
            q[0, pl.ds(pl.multiple_of(x * rows, rows), rows), :] = block

    loads[1].wait()
    loads[2].wait()
    d_sends = []
    for d in (2, 1, 3, 0):
        p = lax.rem(x + d, nx)
        cols = pl.ds(pl.multiple_of(p * width, width), width)
        block = nt(cot[...], wout[cols, :]).astype(BF16)
        if d:
            ds_[d] = block
            d_sends.append(
                send(ds_.at[d], do.at[0, pl.ds(pl.multiple_of(x * rows, rows), rows), :], s_d.at[d], r_d.at[d], (c, p))
            )
        else:
            do[0, pl.ds(pl.multiple_of(x * rows, rows), rows), :] = block

    for d, copy in sorted(kv_sends, key=lambda item: (1, 3, 2).index(item[0])):
        copy.wait_recv()
        forward(d)
    for copy in q_sends:
        copy.wait_recv()
    qf = send(q.at[0], q.at[1], s_f.at[0], r_f.at[0], (behind, x))
    for copy in d_sends:
        copy.wait_recv()
    df = send(do.at[0], do.at[1], s_f.at[1], r_f.at[1], (behind, x))
    for _, copy in kv_sends:
        copy.wait_send()
    for copy in q_sends + d_sends:
        copy.wait_send()

    half = lax.broadcasted_iota(I32, (seq, 128), 1) // HD

    def split_heads(src, dst, qi):
        for h in range(4):
            block = src[qi, :, (h // 2) * 128 : (h // 2) * 128 + 128].astype(F32)
            dst[qi, h] = jnp.where(half == h % 2, block, 0.0).astype(BF16)

    def turn(slot):
        kt[slot] = kv[slot, :, 0:width].astype(F32).T.astype(BF16)
        vt[slot] = kv[slot, :, width : 2 * width].astype(F32).T.astype(BF16)

    ot[...] = jnp.zeros_like(ot)
    tot[...] = jnp.zeros_like(tot)
    dqt[...] = jnp.zeros_like(dqt)
    dkv[...] = jnp.zeros_like(dkv)

    scale = HD ** -0.5
    scale2 = scale * math.log2(math.e)
    kc = 256
    k_iota = lax.broadcasted_iota(I32, (kc, seq), 0)
    q_iota = lax.broadcasted_iota(I32, (kc, seq), 1)

    def attend(block, qi, slot, distance, diag=False):
        def step(i, carry):
            hp, part = i // 2, lax.rem(i, 2)
            k0 = pl.multiple_of(part * kc, kc)
            lanes = pl.ds(pl.multiple_of(hp * 128, 128), 128)
            keys = kv[slot, pl.ds(k0, kc), lanes]
            q_shard = jnp.where(qi == 0, c, ahead)
            k_pos = (q_shard - distance) * seq + k0 + k_iota
            ok = k_pos >= starts[qi, 0:1, :]
            if diag:
                ok = ok & (k0 + k_iota <= q_iota)
            for s in (0, 1):
                h = hp * 2 + s
                score = nt(keys, qm[qi, h])
                e = jnp.where(ok, jnp.exp2(score * scale2), 0.0)
                e_ref[block, h, pl.ds(k0, kc), :] = e
                tot[qi, h] += jnp.sum(e, axis=0, keepdims=True)
                head_rows = pl.ds(pl.multiple_of(h * HD, HD), HD)
                ot[qi, head_rows, :] += nn(vt[slot, head_rows, pl.ds(k0, kc)], e.astype(BF16))
            return carry

        lax.fori_loop(0, 4, step, 0)

    def grads(block, qi, slot, hp):
        lanes = pl.ds(hp * 128, 128)

        def step(part, carry):
            k0 = pl.multiple_of(part * kc, kc)
            values = kv[slot, pl.ds(k0, kc), pl.ds(width + hp * 128, 128)]
            for s in (0, 1):
                h = hp * 2 + s
                prob = e_ref[block, h, pl.ds(k0, kc), :] * stat[qi, h : h + 1, :]
                d_prob = nt(values, dm[qi, h])
                d_score = (prob * (d_prob - stat[qi, 4 + h : 5 + h, :])).astype(BF16)
                dkv[slot, hp, pl.ds(k0, kc), 128:256] += nn(prob.astype(BF16), dm[qi, h])
                dkv[slot, hp, pl.ds(k0, kc), 0:128] += nn(d_score, qm[qi, h])
                head_rows = pl.ds(h * HD, HD)
                dqt[qi, head_rows, :] += nn(kt[slot, head_rows, pl.ds(k0, kc)], d_score)
            return carry

        lax.fori_loop(0, seq // kc, step, 0)

    split_heads(q, qm, 0)
    turn(OWN)
    attend(0, 0, OWN, 0, diag=True)
    pp_sends = {}
    for d in (0, 1, 3, 2):
        z_sends[d].wait_recv()
        at = piece(d)
        pp_sends[d] = send(kv.at[PREV, at, :], kv.at[PREVX, at, :], s_pp.at[d], r_pp.at[d], (pair, x))
    qf.wait_recv()
    split_heads(q, qm, 1)
    turn(PREV)

    def near_far(qi, carry):
        attend(1 + qi, qi, PREV, 2 + 2 * qi)
        return carry

    lax.fori_loop(0, 2, near_far, 0)
    for d in range(nx):
        pp_sends[d].wait_recv()
        sp_sends[d].wait_recv()
    turn(PREVX)
    turn(PAIR)
    far = 1 - core
    far_slot = PREVX + core

    def crossed(j, carry):
        attend(3 + j, j * far, PREVX + j * core, jnp.where(j == 0, 1 + 2 * core, 3 - 2 * core))
        return carry

    lax.fori_loop(0, 2, crossed, 0)
    of_s[...] = ot[1].astype(BF16)
    for h in range(4):
        tf_s[h : h + 1, :] = tot[1, h]
        tf_s[4 + h : 5 + h, :] = tot[1, h]
    of = send(of_s, of_r, s_f.at[2], r_f.at[2], (ahead, x))
    tf = send(tf_s, tf_r, s_f.at[3], r_f.at[3], (ahead, x))
    df.wait_recv()
    split_heads(do, dm, 0)
    split_heads(do, dm, 1)
    tf.wait_recv()
    of.wait_recv()

    for h in range(4):
        head_rows = slice(h * HD, (h + 1) * HD)
        total = tot[0, h] + tf_r[h : h + 1, :]
        inverse = 1.0 / total
        context = ((ot[0, head_rows, :] + of_r[head_rows, :].astype(F32)) / total).astype(BF16)
        ctxt[head_rows, :] = context.astype(F32)
        stat[0, h : h + 1, :] = inverse
    d_turned = do[0].astype(F32).T
    product = d_turned * ctxt[...]
    for h in range(4):
        stat[0, 4 + h : 5 + h, :] = jnp.sum(product[h * HD : (h + 1) * HD, :], axis=0, keepdims=True)
    st_s[...] = stat[0]
    st = send(st_s, stat.at[1], s_f.at[4], r_f.at[4], (behind, x))
    cx_sends = []
    for d in (2, 1, 3, 0):
        p = lax.rem(x + d, nx)
        block = ctxt[:, pl.ds(pl.multiple_of(p * rows, rows), rows)].T.astype(BF16)
        if d:
            cxs[d] = block
            cx_sends.append(send(cxs.at[d], cx.at[x], s_cx.at[d], r_cx.at[d], (c, p)))
        else:
            cx[x] = block
    st.wait_recv()

    sent = []
    for hp in (0, 1):

        def crossed_grads(j, carry):
            grads(3 + j, j * far, PREVX + j * core, hp)
            return carry

        lax.fori_loop(0, 2, crossed_grads, 0)
        pp_s[hp] = dkv[PREVX, hp].astype(BF16)
        ppg = send(pp_s.at[hp], pp_r.at[hp], s_gr.at[hp], r_gr.at[hp], (pair, x))
        sp_s[hp] = dkv[PAIR, hp].astype(BF16)
        spg = send(sp_s.at[hp], sp_r.at[hp], s_gr.at[2 + hp], r_gr.at[2 + hp], (pair, x))

        def near_far_grads(qi, carry):
            grads(1 + qi, qi, PREV, hp)
            return carry

        lax.fori_loop(0, 2, near_far_grads, 0)
        dq_rows = pl.ds(hp * 128, 128)
        dqf_s[dq_rows, :] = dqt[1, dq_rows, :].astype(BF16)
        dqf = send(dqf_s.at[dq_rows, :], dqf_r.at[dq_rows, :], s_gr.at[6 + hp], r_gr.at[6 + hp], (ahead, x))
        ppg.wait_recv()
        ps_s[hp] = (dkv[PREV, hp] + pp_r[hp].astype(F32)).astype(BF16)
        psg = send(ps_s.at[hp], ps_r.at[hp], s_gr.at[4 + hp], r_gr.at[4 + hp], (behind, x))
        sent.append((ppg, spg, dqf, psg))
    for hp in (0, 1):
        grads(0, 0, OWN, hp)

    acc = nn(cx[x], wout[pl.ds(pl.multiple_of(x * width, width), width), :])
    for d, copy in zip((2, 1, 3), cx_sends):
        copy.wait_recv()
        src = lax.rem(x + nx - d, nx)
        acc = acc + nn(cx[src], wout[pl.ds(pl.multiple_of(src * width, width), width), :])
    att_out[...] = acc.astype(BF16)

    for hp in (0, 1):
        ppg, spg, dqf, psg = sent[hp]
        spg.wait_recv()
        psg.wait_recv()
        dqf.wait_recv()
        dkv[OWN, hp] = dkv[OWN, hp] + ps_r[hp].astype(F32) + sp_r[hp].astype(F32)
    dqt[0] = dqt[0] + dqf_r[...].astype(F32)
    g_sends = []
    for d in (2, 1, 3, 0):
        p = lax.rem(x + d, nx)
        at = pl.ds(pl.multiple_of(p * rows, rows), rows)
        parts = [(dqt[0, :, at] * scale).T.astype(BF16)]
        parts += [(dkv[OWN, hp, at, 0:128] * scale).astype(BF16) for hp in (0, 1)]
        parts += [dkv[OWN, hp, at, 128:256].astype(BF16) for hp in (0, 1)]
        column = 0
        for part in parts:
            gs[d, :, column : column + part.shape[1]] = part
            column += part.shape[1]
        if d:
            g_sends.append((d, send(gs.at[d], g.at[d], s_g.at[d], r_g.at[d], (c, p))))

    acc = None
    for d, copy in [(0, None)] + g_sends:
        if copy is not None:
            copy.wait_recv()
        src = lax.rem(x + nx - d, nx)
        cols = pl.ds(pl.multiple_of(src * width, width), width)
        for i in range(3):
            block = (g if d else gs)[d, :, i * width : (i + 1) * width]
            term = nt(block, w3[i, :, cols])
            acc = term if acc is None else acc + term
    gm[pl.ds(HALO, rows), :] = acc.astype(BF16)
    g_up = send(gm.at[pl.ds(rows, HALO), :], gm.at[pl.ds(0, HALO), :], s_h.at[2], r_h.at[2], (up_c, up_x))
    g_dn = send(gm.at[pl.ds(HALO, HALO), :], gm.at[pl.ds(HALO + rows, HALO), :], s_h.at[3], r_h.at[3], (dn_c, dn_x))
    g_up.wait()
    g_dn.wait()
    ext32[...] = gm[...].astype(F32)
    convolve(ig_out, True)

    for d in range(nx):
        z_sends[d].wait_send()
        sp_sends[d].wait_send()
        pp_sends[d].wait_send()
    for copy in [qf, df, of, tf, st] + cx_sends + [copy for _, copy in g_sends]:
        copy.wait_send()
    for group in sent:
        for copy in group:
            copy.wait_send()


def on_device(tokens, conv_kernel, w_qkv, w_out, lengths, cotangent):
    rows, model = tokens.shape
    vmem = lambda shape, dtype: pltpu.VMEM(shape, dtype)
    dma = lambda count: pltpu.SemaphoreType.DMA((count,))
    scratch = [
        vmem((rows + 2 * HALO, model), BF16),
        vmem((rows + 2 * HALO, model), F32),
        vmem((KS, rows, 128), F32),
        vmem((rows, model), BF16),
        vmem((3, model, model), BF16),
        vmem((model, model), BF16),
        vmem((rows, model), BF16),
        vmem((4, rows, 512), BF16),
        vmem((4, rows, 256), BF16),
        vmem((4, rows, 256), BF16),
        vmem((4, 512, 512), BF16),
        vmem((2, 512, 256), BF16),
        vmem((2, 512, 256), BF16),
        vmem((4, 256, 512), BF16),
        vmem((4, 256, 512), BF16),
        vmem((2, 4, 512, 128), BF16),
        vmem((2, 4, 512, 128), BF16),
        vmem((2, 8, 512), I32),
        vmem((5, 4, 512, 512), F32),
        vmem((2, 256, 512), F32),
        vmem((2, 4, 1, 512), F32),
        vmem((256, 512), BF16),
        vmem((256, 512), BF16),
        vmem((8, 512), F32),
        vmem((8, 512), F32),
        vmem((2, 8, 512), F32),
        vmem((8, 512), F32),
        vmem((256, 512), F32),
        vmem((4, rows, 256), BF16),
        vmem((4, rows, 256), BF16),
        vmem((4, 2, 512, 256), F32),
        vmem((2, 256, 512), F32),
        vmem((2, 512, 256), BF16),
        vmem((2, 512, 256), BF16),
        vmem((2, 512, 256), BF16),
        vmem((2, 512, 256), BF16),
        vmem((2, 512, 256), BF16),
        vmem((2, 512, 256), BF16),
        vmem((256, 512), BF16),
        vmem((256, 512), BF16),
        vmem((4, rows, 768), BF16),
        vmem((4, rows, 768), BF16),
        vmem((rows + 2 * HALO, model), BF16),
        dma(6),
    ]
    for count in (4, 4, 4, 4, 4, 4, 4, 5, 4, 8, 4):
        scratch += [dma(count), dma(count)]
    whole = pl.BlockSpec(memory_space=pltpu.VMEM)
    anywhere = pl.BlockSpec(memory_space=pl.ANY)
    out = jax.ShapeDtypeStruct((rows, model), BF16)
    return pl.pallas_call(
        functools.partial(layer_kernel, lax.axis_size("ctx")),
        out_shape=(out, out),
        in_specs=[anywhere, anywhere, anywhere, anywhere, whole, pl.BlockSpec(memory_space=pltpu.SMEM)],
        out_specs=(whole, whole),
        scratch_shapes=scratch,
        compiler_params=pltpu.CompilerParams(
            collective_id=0, has_side_effects=True, vmem_limit_bytes=66_000_000
        ),
    )(tokens, cotangent, w_qkv, w_out, conv_kernel, lengths)


def solution(mesh):
    placed = (P(("ctx", "head"), None), P(), P(), P(), P(), P(("ctx", "head"), None))
    return jax.shard_map(
        on_device,
        mesh=mesh,
        in_specs=placed,
        out_specs=(P(("ctx", "head"), None), P(("ctx", "head"), None)),
        check_vma=False,
    )
```

```python
import functools
import math

import jax
import jax.numpy as jnp
from jax import lax
from jax.experimental import pallas as pl
from jax.experimental.pallas import tpu as pltpu
from jax.sharding import PartitionSpec as P

HD = 64
KS = 7
HALO = 16
OWN, PREV, PREVX, PAIR = 0, 1, 2, 3
MESH = pl.DeviceIdType.MESH
F32, BF16, I32 = jnp.float32, jnp.bfloat16, jnp.int32


def nt(a, b):
    return lax.dot_general(a, b, (((1,), (1,)), ((), ())), preferred_element_type=F32)


def nn(a, b):
    return jnp.dot(a, b, preferred_element_type=F32)


def layer_kernel(
    n_ctx,
    tok_hbm,
    cot_hbm,
    wqkv_hbm,
    wout_hbm,
    convk,
    lens,
    att_out,
    ig_out,
    ext,
    ext32,
    cmask,
    cot,
    w3,
    wout,
    mixed,
    kvs,
    qs,
    ds_,
    kv,
    q,
    do,
    kt,
    vt,
    qm,
    dm,
    starts,
    e_ref,
    ot,
    tot,
    of_s,
    of_r,
    tf_s,
    tf_r,
    stat,
    st_s,
    ctxt,
    cxs,
    cx,
    dkv,
    dqt,
    pp_s,
    pp_r,
    sp_s,
    sp_r,
    ps_s,
    ps_r,
    dqf_s,
    dqf_r,
    gs,
    g,
    gm,
    gacc,
    ld,
    s_h,
    r_h,
    s_kv,
    r_kv,
    s_z,
    r_z,
    s_sp,
    r_sp,
    s_pp,
    r_pp,
    s_q,
    r_q,
    s_d,
    r_d,
    s_f,
    r_f,
    s_cx,
    r_cx,
    s_gr,
    r_gr,
    s_g,
    r_g,
):
    c, x = lax.axis_index("ctx"), lax.axis_index("head")
    core = lax.rem(c, 2)
    ahead = lax.rem(c + 2, n_ctx)
    behind = lax.rem(c + n_ctx - 2, n_ctx)
    pair = c + 1 - 2 * core
    rows, width = 128, 256
    seq = 512
    nx = 4
    model = 1024

    up_x = lax.rem(x + 1, nx)
    up_c = lax.rem(c + (x + 1) // nx, n_ctx)
    dn_x = lax.rem(x + nx - 1, nx)
    dn_c = lax.rem(c + n_ctx - (nx - x) // nx, n_ctx)

    loads = [
        pltpu.make_async_copy(tok_hbm, ext.at[pl.ds(HALO, rows), :], ld.at[0]),
        pltpu.make_async_copy(cot_hbm, cot, ld.at[1]),
        pltpu.make_async_copy(wout_hbm, wout, ld.at[2]),
        pltpu.make_async_copy(wqkv_hbm.at[:, pl.ds(model, model)], w3.at[1], ld.at[3]),
        pltpu.make_async_copy(wqkv_hbm.at[:, pl.ds(2 * model, model)], w3.at[2], ld.at[4]),
        pltpu.make_async_copy(wqkv_hbm.at[:, pl.ds(0, model)], w3.at[0], ld.at[5]),
    ]
    for i in (0, 1, 2, 3, 4, 5):
        loads[i].start()

    barrier = pltpu.get_barrier_semaphore()
    peers = [(c, lax.rem(x + d, nx)) for d in (1, 2, 3)]
    peers += [(ahead, x), (behind, x), (pair, x), (up_c, up_x), (dn_c, dn_x)]
    for peer in peers:
        pl.semaphore_signal(barrier, inc=1, device_id=peer, device_id_type=MESH)

    ends = []
    run = jnp.int32(0)
    for i in range(lens.shape[0]):
        run = run + lens[i]
        ends.append(run)
    lane = lax.broadcasted_iota(I32, (8, seq), 1)
    for qi, shard in ((0, c), (1, ahead)):
        pos = shard * seq + lane
        first = jnp.zeros((8, seq), I32)
        for end in ends:
            first = jnp.where(pos >= end, end, first)
        starts[qi] = first
    row_pos = (c * nx + x) * rows + lax.broadcasted_iota(I32, (rows, 128), 0)
    first = jnp.zeros((rows, 128), I32)
    for end in ends:
        first = jnp.where(row_pos >= end, end, first)
    last = jnp.zeros((rows, 128), I32)
    for end in reversed(ends):
        last = jnp.where(row_pos < end, end, last)
    for t in range(KS):
        near = row_pos + (t - KS // 2)
        cmask[t] = jnp.where((near >= first) & (near < last), 1.0, 0.0).astype(F32)
    ot[...] = jnp.zeros_like(ot)
    tot[...] = jnp.zeros_like(tot)
    dqt[...] = jnp.zeros_like(dqt)
    dkv[...] = jnp.zeros_like(dkv)

    def columns(p):
        return pl.ds(pl.multiple_of(p * width, width), width)

    def row_block(p):
        return pl.ds(pl.multiple_of(p * rows, rows), rows)

    peer_at = [lax.rem(x + d, nx) for d in range(nx)]
    source = [lax.rem(x + nx - d, nx) for d in range(nx)]
    mine = row_block(x)

    loads[1].wait()
    loads[2].wait()
    for d in (2, 1, 3, 0):
        block = nt(cot[...], wout[columns(peer_at[d]), :]).astype(BF16)
        if d:
            ds_[d] = block
        else:
            do[0, mine, :] = block
    loads[0].wait()
    pl.semaphore_wait(barrier, len(peers))

    started = []

    def send(src, dst, ss, rs, peer):
        copy = pltpu.make_async_remote_copy(
            src_ref=src, dst_ref=dst, send_sem=ss, recv_sem=rs, device_id=peer, device_id_type=MESH
        )
        copy.start()
        started.append(copy)
        return copy

    def exchange_edges(buf, base):
        up = send(
            buf.at[pl.ds(rows, HALO), :], buf.at[pl.ds(0, HALO), :],
            s_h.at[base], r_h.at[base], (up_c, up_x),
        )
        down = send(
            buf.at[pl.ds(HALO, HALO), :], buf.at[pl.ds(HALO + rows, HALO), :],
            s_h.at[base + 1], r_h.at[base + 1], (dn_c, dn_x),
        )
        return up, down

    def convolve(buf, edges, out, flip):
        def part(at, count):
            def chunk(i, carry):
                lanes = pl.ds(pl.multiple_of(i * 128, 128), 128)
                acc = ext32[pl.ds(HALO + at, count), lanes]
                for t in range(KS):
                    tap = convk[pl.ds(KS - 1 - t if flip else t, 1), lanes]
                    near = ext32[pl.ds(HALO + at - KS // 2 + t, count), lanes]
                    acc = acc + tap * near * cmask[t, pl.ds(at, count), :]
                out[pl.ds(at, count), lanes] = acc.astype(BF16)
                return carry

            lax.fori_loop(0, model // 128, chunk, 0)

        inner = pl.ds(HALO, rows)
        ext32[inner, :] = buf[inner, :].astype(F32)
        part(HALO, rows - 2 * HALO)
        for edge in edges:
            edge.wait_recv()
        for side in (0, HALO + rows):
            ext32[pl.ds(side, HALO), :] = buf[pl.ds(side, HALO), :].astype(F32)
        part(0, HALO)
        part(rows - HALO, HALO)

    edges = exchange_edges(ext, 0)
    d_sends = [
        send(ds_.at[d], do.at[0, mine, :], s_d.at[d], r_d.at[d], (c, peer_at[d])) for d in (2, 1, 3)
    ]
    convolve(ext, edges, mixed, False)

    loads[3].wait()
    loads[4].wait()
    kv_sends = {}
    for d in (2, 1, 3, 0):
        cols = columns(peer_at[d])
        for part in (0, 1):
            block = nn(mixed[...], w3[1 + part, :, cols]).astype(BF16)
            lanes = slice(part * width, (part + 1) * width)
            if d:
                kvs[d, :, lanes] = block
            else:
                kv[OWN, mine, lanes] = block
        if d:
            kv_sends[d] = send(kvs.at[d], kv.at[OWN, mine, :], s_kv.at[d], r_kv.at[d], (c, peer_at[d]))

    z_sends, sp_sends, pp_sends = {}, {}, {}

    def forward(d):
        at = row_block(source[d])
        z_sends[d] = send(kv.at[OWN, at, :], kv.at[PREV, at, :], s_z.at[d], r_z.at[d], (ahead, x))
        sp_sends[d] = send(kv.at[OWN, at, :], kv.at[PAIR, at, :], s_sp.at[d], r_sp.at[d], (pair, x))

    forward(0)

    loads[5].wait()
    q_sends = []
    for d in (2, 1, 3, 0):
        block = nn(mixed[...], w3[0, :, columns(peer_at[d])]).astype(BF16)
        if d:
            qs[d] = block
            q_sends.append(send(qs.at[d], q.at[0, mine, :], s_q.at[d], r_q.at[d], (c, peer_at[d])))
        else:
            q[0, mine, :] = block

    for d in (1, 3, 2):
        kv_sends[d].wait_recv()
        forward(d)
    for copy in q_sends:
        copy.wait_recv()
    qf = send(q.at[0], q.at[1], s_f.at[0], r_f.at[0], (behind, x))
    for copy in d_sends:
        copy.wait_recv()
    df = send(do.at[0], do.at[1], s_f.at[1], r_f.at[1], (behind, x))

    half = lax.broadcasted_iota(I32, (seq, 128), 1) // HD

    def split_heads(src, dst, qi):
        for h in range(4):
            block = src[qi, :, (h // 2) * 128 : (h // 2) * 128 + 128].astype(F32)
            dst[qi, h] = jnp.where(half == h % 2, block, 0.0).astype(BF16)

    def turn(slot):
        kt[slot] = kv[slot, :, 0:width].astype(F32).T.astype(BF16)
        vt[slot] = kv[slot, :, width : 2 * width].astype(F32).T.astype(BF16)

    scale = HD ** -0.5
    scale2 = scale * math.log2(math.e)
    kc = 256
    FULL = ((0, 0, seq), (kc, 0, seq))
    LOWER = ((0, 0, seq), (kc, kc, seq - kc))
    UPPER = ((0, 0, kc), (kc, 0, seq))

    def attend(block, qi, slot, distance, parts):
        base = (jnp.where(qi == 0, c, ahead) - distance) * seq

        def tile(hp, k0, q0, queries):
            lanes = pl.ds(pl.multiple_of(hp * 128, 128), 128)
            at = pl.ds(q0, queries)
            keys = kv[slot, pl.ds(k0, kc), lanes]
            k_iota = lax.broadcasted_iota(I32, (kc, queries), 0)
            ok = base + k0 + k_iota >= starts[qi, 0:1, at]
            if parts is LOWER:
                q_iota = lax.broadcasted_iota(I32, (kc, queries), 1)
                ok = ok & (k0 + k_iota <= q0 + q_iota)
            for s in (0, 1):
                h = hp * 2 + s
                score = nt(keys, qm[qi, h, at, :])
                e = jnp.where(ok, jnp.exp2(score * scale2), 0.0)
                e_ref[block, h, pl.ds(k0, kc), at] = e
                tot[qi, h, :, at] += jnp.sum(e, axis=0, keepdims=True)
                head_rows = pl.ds(pl.multiple_of(h * HD, HD), HD)
                ot[qi, head_rows, at] += nn(vt[slot, head_rows, pl.ds(k0, kc)], e.astype(BF16))

        if parts is FULL:

            def step(i, carry):
                tile(i // 2, pl.multiple_of(lax.rem(i, 2) * kc, kc), 0, seq)
                return carry

            lax.fori_loop(0, 4, step, 0)
        else:

            def step(hp, carry):
                for part in parts:
                    tile(hp, *part)
                return carry

            lax.fori_loop(0, 2, step, 0)

    def grads(block, qi, slot, hp, parts):
        def tile(k0, q0, queries):
            at = pl.ds(q0, queries)
            keys_at = pl.ds(k0, kc)
            values = kv[slot, keys_at, pl.ds(width + hp * 128, 128)]
            for s in (0, 1):
                h = hp * 2 + s
                prob = e_ref[block, h, keys_at, at] * stat[qi, h : h + 1, at]
                d_prob = nt(values, dm[qi, h, at, :])
                d_score = (prob * (d_prob - stat[qi, 4 + h : 5 + h, at])).astype(BF16)
                dkv[slot, hp, keys_at, 128:256] += nn(prob.astype(BF16), dm[qi, h, at, :])
                dkv[slot, hp, keys_at, 0:128] += nn(d_score, qm[qi, h, at, :])
                head_rows = pl.ds(h * HD, HD)
                dqt[qi, head_rows, at] += nn(kt[slot, head_rows, keys_at], d_score)

        if parts is FULL:

            def step(part, carry):
                tile(pl.multiple_of(part * kc, kc), 0, seq)
                return carry

            lax.fori_loop(0, seq // kc, step, 0)
        else:
            for part in parts:
                tile(*part)

    far = 1 - core
    split_heads(q, qm, 0)
    turn(OWN)
    attend(0, 0, OWN, 0, LOWER)
    for d in (0, 1, 3, 2):
        z_sends[d].wait_recv()
        at = row_block(source[d])
        pp_sends[d] = send(kv.at[PREV, at, :], kv.at[PREVX, at, :], s_pp.at[d], r_pp.at[d], (pair, x))
    qf.wait_recv()
    split_heads(q, qm, 1)
    turn(PREV)
    attend(2, 1, PREV, 4, UPPER)
    for d in range(nx):
        pp_sends[d].wait_recv()
        sp_sends[d].wait_recv()
    turn(PREVX)
    turn(PAIR)
    attend(4, far, PREVX + core, 3 - 2 * core, FULL)
    of_s[...] = ot[1].astype(BF16)
    for h in range(4):
        tf_s[h : h + 1, :] = tot[1, h]
        tf_s[4 + h : 5 + h, :] = tot[1, h]
    tf = send(tf_s, tf_r, s_f.at[3], r_f.at[3], (ahead, x))
    of = send(of_s, of_r, s_f.at[2], r_f.at[2], (ahead, x))

    def near_blocks(j, carry):
        attend(1 + 2 * j, 0, PREV + j, 2 - j * (1 - 2 * core), FULL)
        return carry

    lax.fori_loop(0, 2, near_blocks, 0)
    df.wait_recv()
    split_heads(do, dm, 0)
    split_heads(do, dm, 1)
    d_turned = do[0].astype(F32).T
    tf.wait_recv()
    of.wait_recv()

    for h in range(4):
        head_rows = slice(h * HD, (h + 1) * HD)
        total = tot[0, h] + tf_r[h : h + 1, :]
        context = ((ot[0, head_rows, :] + of_r[head_rows, :].astype(F32)) / total).astype(BF16)
        context = context.astype(F32)
        ctxt[head_rows, :] = context
        stat[0, h : h + 1, :] = 1.0 / total
        stat[0, 4 + h : 5 + h, :] = jnp.sum(d_turned[head_rows, :] * context, axis=0, keepdims=True)
    st_s[...] = stat[0]
    st = send(st_s, stat.at[1], s_f.at[4], r_f.at[4], (behind, x))
    cx_sends = {}
    for d in (2, 1, 3, 0):
        block = ctxt[:, row_block(peer_at[d])].T.astype(BF16)
        if d:
            cxs[d] = block
            cx_sends[d] = send(cxs.at[d], cx.at[d], s_cx.at[d], r_cx.at[d], (c, peer_at[d]))
        else:
            cx[0] = block

    sent = []
    for hp in (0, 1):

        def near_grads(j, carry):
            grads(1 + 2 * j, 0, PREV + j, hp, FULL)
            return carry

        lax.fori_loop(0, 2, near_grads, 0)
        if hp == 0:
            st.wait_recv()
        grads(4, far, PREVX + core, hp, FULL)
        pp_s[hp] = dkv[PREVX, hp].astype(BF16)
        ppg = send(pp_s.at[hp], pp_r.at[hp], s_gr.at[hp], r_gr.at[hp], (pair, x))
        sp_s[hp] = dkv[PAIR, hp].astype(BF16)
        spg = send(sp_s.at[hp], sp_r.at[hp], s_gr.at[2 + hp], r_gr.at[2 + hp], (pair, x))
        grads(2, 1, PREV, hp, UPPER)
        dq_rows = pl.ds(hp * 128, 128)
        dqf_s[dq_rows, :] = dqt[1, dq_rows, :].astype(BF16)
        dqf = send(dqf_s.at[dq_rows, :], dqf_r.at[dq_rows, :], s_gr.at[6 + hp], r_gr.at[6 + hp], (ahead, x))
        ppg.wait_recv()
        ps_s[hp] = (dkv[PREV, hp] + pp_r[hp].astype(F32)).astype(BF16)
        psg = send(ps_s.at[hp], ps_r.at[hp], s_gr.at[4 + hp], r_gr.at[4 + hp], (behind, x))
        sent.append((spg, dqf, psg))
    for hp in (0, 1):
        grads(0, 0, OWN, hp, LOWER)

    g_sends = {}

    def give(group):
        if group == 1:
            for _, dqf, _ in sent:
                dqf.wait_recv()
            dqt[0] = (dqt[0] + dqf_r[...].astype(F32)) * scale
        else:
            hp = group // 2
            spg, _, psg = sent[hp]
            spg.wait_recv()
            psg.wait_recv()
        for d in (2, 1, 3, 0):
            at = row_block(peer_at[d])
            out = gs.at[group, d] if d else g.at[group, 0]
            if group == 1:
                out[...] = dqt[0, :, at].T.astype(BF16)
            else:
                hp = group // 2
                total = dkv[OWN, hp, at, :] + ps_r[hp, at, :].astype(F32) + sp_r[hp, at, :].astype(F32)
                out[:, 0:128] = (total[:, 0:128] * scale).astype(BF16)
                out[:, 128:256] = total[:, 128:256].astype(BF16)
            if d:
                slot = group * nx + d
                g_sends[group, d] = send(
                    gs.at[group, d], g.at[group, d], s_g.at[slot], r_g.at[slot], (c, peer_at[d])
                )

    def take(group, d):
        if d:
            g_sends[group, d].wait_recv()
        if group == 1:
            return nt(g[1, d], w3[0, :, columns(source[d])])
        cols = pl.ds(pl.multiple_of(source[d] * width + (group // 2) * 128, 128), 128)
        return nt(g[group, d, :, 0:128], w3[1, :, cols]) + nt(g[group, d, :, 128:256], w3[2, :, cols])

    give(0)
    acc = nn(cx[0], wout[columns(x), :])
    for d in (1, 3, 2):
        cx_sends[d].wait_recv()
        acc = acc + nn(cx[d], wout[columns(source[d]), :])
    att_out[...] = acc.astype(BF16)
    give(1)
    gacc[...] = take(0, 0) + take(1, 0)
    for d in (1, 3, 2):
        gacc[...] += take(0, d)
    give(2)
    for d in (1, 3, 2):
        gacc[...] += take(1, d)
    gacc[...] += take(2, 0)
    for d in (1, 3, 2):
        gacc[...] += take(2, d)
    gm[pl.ds(HALO, rows), :] = gacc[...].astype(BF16)
    convolve(gm, exchange_edges(gm, 2), ig_out, True)

    for copy in started:
        copy.wait_send()


def on_device(tokens, conv_kernel, w_qkv, w_out, lengths, cotangent):
    rows, model = tokens.shape
    vmem = lambda shape, dtype: pltpu.VMEM(shape, dtype)
    dma = lambda count: pltpu.SemaphoreType.DMA((count,))
    scratch = [
        vmem((rows + 2 * HALO, model), BF16),
        vmem((rows + 2 * HALO, model), F32),
        vmem((KS, rows, 128), F32),
        vmem((rows, model), BF16),
        vmem((3, model, model), BF16),
        vmem((model, model), BF16),
        vmem((rows, model), BF16),
        vmem((4, rows, 512), BF16),
        vmem((4, rows, 256), BF16),
        vmem((4, rows, 256), BF16),
        vmem((4, 512, 512), BF16),
        vmem((2, 512, 256), BF16),
        vmem((2, 512, 256), BF16),
        vmem((4, 256, 512), BF16),
        vmem((4, 256, 512), BF16),
        vmem((2, 4, 512, 128), BF16),
        vmem((2, 4, 512, 128), BF16),
        vmem((2, 8, 512), I32),
        vmem((5, 4, 512, 512), F32),
        vmem((2, 256, 512), F32),
        vmem((2, 4, 1, 512), F32),
        vmem((256, 512), BF16),
        vmem((256, 512), BF16),
        vmem((8, 512), F32),
        vmem((8, 512), F32),
        vmem((2, 8, 512), F32),
        vmem((8, 512), F32),
        vmem((256, 512), F32),
        vmem((4, rows, 256), BF16),
        vmem((4, rows, 256), BF16),
        vmem((4, 2, 512, 256), F32),
        vmem((2, 256, 512), F32),
        vmem((2, 512, 256), BF16),
        vmem((2, 512, 256), BF16),
        vmem((2, 512, 256), BF16),
        vmem((2, 512, 256), BF16),
        vmem((2, 512, 256), BF16),
        vmem((2, 512, 256), BF16),
        vmem((256, 512), BF16),
        vmem((256, 512), BF16),
        vmem((3, 4, rows, 256), BF16),
        vmem((3, 4, rows, 256), BF16),
        vmem((rows + 2 * HALO, model), BF16),
        vmem((rows, model), F32),
        dma(6),
    ]
    for count in (4, 4, 4, 4, 4, 4, 4, 5, 4, 8, 12):
        scratch += [dma(count), dma(count)]
    whole = pl.BlockSpec(memory_space=pltpu.VMEM)
    anywhere = pl.BlockSpec(memory_space=pl.ANY)
    out = jax.ShapeDtypeStruct((rows, model), BF16)
    return pl.pallas_call(
        functools.partial(layer_kernel, lax.axis_size("ctx")),
        out_shape=(out, out),
        in_specs=[anywhere, anywhere, anywhere, anywhere, whole, pl.BlockSpec(memory_space=pltpu.SMEM)],
        out_specs=(whole, whole),
        scratch_shapes=scratch,
        compiler_params=pltpu.CompilerParams(
            collective_id=0, has_side_effects=True, vmem_limit_bytes=66_000_000
        ),
    )(tokens, cotangent, w_qkv, w_out, conv_kernel, lengths)


def solution(mesh):
    placed = (P(("ctx", "head"), None), P(), P(), P(), P(), P(("ctx", "head"), None))
    return jax.shard_map(
        on_device,
        mesh=mesh,
        in_specs=placed,
        out_specs=(P(("ctx", "head"), None), P(("ctx", "head"), None)),
        check_vma=False,
    )
```

```python
import functools
import math

import jax
import jax.numpy as jnp
from jax import lax
from jax.experimental import pallas as pl
from jax.experimental.pallas import tpu as pltpu
from jax.sharding import PartitionSpec as P

HD = 64
KS = 7
HALO = 16
OWN, PREV, PREVX, PAIR = 0, 1, 2, 3
MESH = pl.DeviceIdType.MESH
F32, BF16, I32 = jnp.float32, jnp.bfloat16, jnp.int32


def nt(a, b):
    return lax.dot_general(a, b, (((1,), (1,)), ((), ())), preferred_element_type=F32)


def nn(a, b):
    return jnp.dot(a, b, preferred_element_type=F32)


def layer_kernel(
    n_ctx,
    tok_hbm,
    cot_hbm,
    wqkv_hbm,
    wout_hbm,
    convk_hbm,
    lens_hbm,
    att_out,
    ig_out,
    ext,
    ext32,
    cmask,
    cot,
    w3,
    wout,
    mixed,
    kvs,
    qs,
    ds_,
    kv,
    q,
    do,
    kt,
    vt,
    qm,
    dm,
    starts,
    e_ref,
    ot,
    tot,
    of_s,
    of_r,
    tf_s,
    tf_r,
    stat,
    st_s,
    ctxt,
    cxs,
    cx,
    dkv,
    dqt,
    pp_s,
    pp_r,
    sp_s,
    sp_r,
    ps_s,
    ps_r,
    dqf_s,
    dqf_r,
    gs,
    g,
    gm,
    gacc,
    convk,
    lens,
    ld,
    s_h,
    r_h,
    s_kv,
    r_kv,
    s_z,
    r_z,
    s_sp,
    r_sp,
    s_pp,
    r_pp,
    s_q,
    r_q,
    s_d,
    r_d,
    s_qf,
    r_qf,
    s_f,
    r_f,
    s_cx,
    r_cx,
    s_gr,
    r_gr,
    s_g,
    r_g,
):
    c, x = lax.axis_index("ctx"), lax.axis_index("head")
    core = lax.rem(c, 2)
    ahead = lax.rem(c + 2, n_ctx)
    behind = lax.rem(c + n_ctx - 2, n_ctx)
    pair = c + 1 - 2 * core
    rows, width = 128, 256
    seq = 512
    nx = 4
    model = 1024

    up_x = lax.rem(x + 1, nx)
    up_c = lax.rem(c + (x + 1) // nx, n_ctx)
    dn_x = lax.rem(x + nx - 1, nx)
    dn_c = lax.rem(c + n_ctx - (nx - x) // nx, n_ctx)

    loads = [
        pltpu.make_async_copy(tok_hbm, ext.at[pl.ds(HALO, rows), :], ld.at[0]),
        pltpu.make_async_copy(lens_hbm, lens, ld.at[1]),
        pltpu.make_async_copy(convk_hbm, convk, ld.at[2]),
        pltpu.make_async_copy(wqkv_hbm.at[:, pl.ds(model, model)], w3.at[1], ld.at[3]),
        pltpu.make_async_copy(wqkv_hbm.at[:, pl.ds(2 * model, model)], w3.at[2], ld.at[4]),
        pltpu.make_async_copy(wqkv_hbm.at[:, pl.ds(0, model)], w3.at[0], ld.at[5]),
        pltpu.make_async_copy(cot_hbm, cot, ld.at[6]),
        pltpu.make_async_copy(wout_hbm, wout, ld.at[7]),
    ]
    barrier = pltpu.get_barrier_semaphore()
    peers = [(c, lax.rem(x + d, nx)) for d in (1, 2, 3)]
    peers += [(ahead, x), (behind, x), (pair, x), (up_c, up_x), (dn_c, dn_x)]
    for peer in peers:
        pl.semaphore_signal(barrier, inc=1, device_id=peer, device_id_type=MESH)
    for load in loads:
        load.start()
    loads[0].wait()
    pl.semaphore_wait(barrier, len(peers))

    started = []

    def send(src, dst, ss, rs, peer):
        copy = pltpu.make_async_remote_copy(
            src_ref=src, dst_ref=dst, send_sem=ss, recv_sem=rs, device_id=peer, device_id_type=MESH
        )
        copy.start()
        started.append(copy)
        return copy

    def exchange_edges(buf, base):
        up = send(
            buf.at[pl.ds(rows, HALO), :], buf.at[pl.ds(0, HALO), :],
            s_h.at[base], r_h.at[base], (up_c, up_x),
        )
        down = send(
            buf.at[pl.ds(HALO, HALO), :], buf.at[pl.ds(HALO + rows, HALO), :],
            s_h.at[base + 1], r_h.at[base + 1], (dn_c, dn_x),
        )
        return up, down

    edges = exchange_edges(ext, 0)

    loads[1].wait()
    ends = []
    run = jnp.int32(0)
    for i in range(lens.shape[0]):
        run = run + lens[i]
        ends.append(run)
    row_pos = (c * nx + x) * rows + lax.broadcasted_iota(I32, (rows, 128), 0)
    first = jnp.zeros((rows, 128), I32)
    for end in ends:
        first = jnp.where(row_pos >= end, end, first)
    last = jnp.zeros((rows, 128), I32)
    for end in reversed(ends):
        last = jnp.where(row_pos < end, end, last)
    for t in range(KS):
        near = row_pos + (t - KS // 2)
        cmask[t] = jnp.where((near >= first) & (near < last), 1.0, 0.0).astype(F32)

    def columns(p):
        return pl.ds(pl.multiple_of(p * width, width), width)

    def row_block(p):
        return pl.ds(pl.multiple_of(p * rows, rows), rows)

    peer_at = [lax.rem(x + d, nx) for d in range(nx)]
    source = [lax.rem(x + nx - d, nx) for d in range(nx)]
    mine = row_block(x)
    ways = (1, 3, 2)

    def convolve(buf, edges, out, flip):
        def part(at, count):
            def chunk(i, carry):
                lanes = pl.ds(pl.multiple_of(i * 128, 128), 128)
                acc = ext32[pl.ds(HALO + at, count), lanes]
                for t in range(KS):
                    tap = convk[pl.ds(KS - 1 - t if flip else t, 1), lanes]
                    near = ext32[pl.ds(HALO + at - KS // 2 + t, count), lanes]
                    acc = acc + tap * near * cmask[t, pl.ds(at, count), :]
                out[pl.ds(at, count), lanes] = acc.astype(BF16)
                return carry

            lax.fori_loop(0, model // 128, chunk, 0)

        inner = pl.ds(HALO, rows)
        ext32[inner, :] = buf[inner, :].astype(F32)
        part(HALO, rows - 2 * HALO)
        for edge in edges:
            edge.wait_recv()
        for side in (0, HALO + rows):
            ext32[pl.ds(side, HALO), :] = buf[pl.ds(side, HALO), :].astype(F32)
        part(0, HALO)
        part(rows - HALO, HALO)

    loads[2].wait()
    convolve(ext, edges, mixed, False)

    kv_sends, z_sends, sp_sends, pp_sends, q_sends, d_sends, qf_sends = {}, {}, {}, {}, {}, {}, {}

    def give_kv(hp, d):
        slot = hp * nx + d
        kv_sends[hp, d] = send(
            kvs.at[d, hp], kv.at[OWN, hp, mine, :], s_kv.at[slot], r_kv.at[slot], (c, peer_at[d])
        )

    def forward(hp, d):
        at, slot = row_block(source[d]), hp * nx + d
        block = kv.at[OWN, hp, at, :]
        z_sends[hp, d] = send(block, kv.at[PREV, hp, at, :], s_z.at[slot], r_z.at[slot], (ahead, x))
        sp_sends[hp, d] = send(block, kv.at[PAIR, hp, at, :], s_sp.at[slot], r_sp.at[slot], (pair, x))

    def forward_pair(hp, d):
        at, slot = row_block(source[d]), hp * nx + d
        pp_sends[hp, d] = send(
            kv.at[PREV, hp, at, :], kv.at[PREVX, hp, at, :], s_pp.at[slot], r_pp.at[slot], (pair, x)
        )

    def forward_q(d):
        at = row_block(source[d])
        qf_sends[d] = send(q.at[0, at, :], q.at[1, at, :], s_qf.at[d], r_qf.at[d], (behind, x))

    loads[3].wait()
    loads[4].wait()
    for d in (2, 1, 3, 0):
        for part in (0, 1):
            block = nn(mixed[...], w3[1 + part, :, columns(peer_at[d])]).astype(BF16)
            for hp in (0, 1):
                piece = block[:, hp * 128 : hp * 128 + 128]
                if d:
                    kvs[d, hp, :, part * 128 : part * 128 + 128] = piece
                else:
                    kv[OWN, hp, mine, part * 128 : part * 128 + 128] = piece
        if d:
            give_kv(0, d)
    forward(0, 0)
    loads[5].wait()
    for d in (2, 1, 3, 0):
        block = nn(mixed[...], w3[0, :, columns(peer_at[d])]).astype(BF16)
        if d:
            qs[d] = block
            q_sends[d] = send(qs.at[d], q.at[0, mine, :], s_q.at[d], r_q.at[d], (c, peer_at[d]))
        else:
            q[0, mine, :] = block
    forward_q(0)
    for d in (2, 1, 3):
        give_kv(1, d)
    for d in ways:
        kv_sends[0, d].wait_recv()
        forward(0, d)
    forward(1, 0)

    loads[6].wait()
    loads[7].wait()
    for d in (2, 1, 3, 0):
        block = nt(cot[...], wout[columns(peer_at[d]), :]).astype(BF16)
        if d:
            ds_[d] = block
            d_sends[d] = send(ds_.at[d], do.at[0, mine, :], s_d.at[d], r_d.at[d], (c, peer_at[d]))
        else:
            do[0, mine, :] = block
    for d in ways:
        q_sends[d].wait_recv()
        forward_q(d)

    lane = lax.broadcasted_iota(I32, (8, seq), 1)
    for qi, shard in ((0, c), (1, ahead)):
        pos = shard * seq + lane
        first = jnp.zeros((8, seq), I32)
        for end in ends:
            first = jnp.where(pos >= end, end, first)
        starts[qi] = first
    half = lax.broadcasted_iota(I32, (seq, 128), 1) // HD

    def split_heads(src, dst, qi):
        for h in range(4):
            block = src[qi, :, (h // 2) * 128 : (h // 2) * 128 + 128].astype(F32)
            dst[qi, h] = jnp.where(half == h % 2, block, 0.0).astype(BF16)

    def turn(slot, hp):
        kt[slot, hp] = kv[slot, hp, :, 0:128].astype(F32).T.astype(BF16)
        vt[slot, hp] = kv[slot, hp, :, 128:256].astype(F32).T.astype(BF16)

    scale = HD ** -0.5
    scale2 = scale * math.log2(math.e)
    kc = 256
    FULL = ((0, 0, seq), (kc, 0, seq))
    LOWER = ((0, 0, seq), (kc, kc, seq - kc))
    UPPER = ((0, 0, kc), (kc, 0, seq))

    def over_parts(parts, tile):
        if parts is FULL:

            def step(part, carry):
                tile(pl.multiple_of(part * kc, kc), 0, seq)
                return carry

            lax.fori_loop(0, seq // kc, step, 0)
        else:
            for part in parts:
                tile(*part)

    def attend(block, qi, slot, distance, parts, hp):
        base = (jnp.where(qi == 0, c, ahead) - distance) * seq

        def tile(k0, q0, queries):
            at = pl.ds(q0, queries)
            keys = kv[slot, hp, pl.ds(k0, kc), 0:128]
            k_iota = lax.broadcasted_iota(I32, (kc, queries), 0)
            ok = base + k0 + k_iota >= starts[qi, 0:1, at]
            if parts is LOWER:
                q_iota = lax.broadcasted_iota(I32, (kc, queries), 1)
                ok = ok & (k0 + k_iota <= q0 + q_iota)
            for s in (0, 1):
                h = hp * 2 + s
                score = nt(keys, qm[qi, h, at, :])
                e = jnp.where(ok, jnp.exp2(score * scale2), 0.0)
                e_ref[block, h, pl.ds(k0, kc), at] = e
                tot[qi, h, :, at] += jnp.sum(e, axis=0, keepdims=True)
                head_rows = pl.ds(s * HD, HD)
                ot[qi, hp, head_rows, at] += nn(vt[slot, hp, head_rows, pl.ds(k0, kc)], e.astype(BF16))

        over_parts(parts, tile)

    def grads(block, qi, slot, hp, parts):
        def tile(k0, q0, queries):
            at = pl.ds(q0, queries)
            keys_at = pl.ds(k0, kc)
            values = kv[slot, hp, keys_at, 128:256]
            for s in (0, 1):
                h = hp * 2 + s
                prob = e_ref[block, h, keys_at, at] * stat[qi, hp, s : s + 1, at]
                d_prob = nt(values, dm[qi, h, at, :])
                d_score = (prob * (d_prob - stat[qi, hp, 4 + s : 5 + s, at])).astype(BF16)
                dkv[slot, hp, keys_at, 128:256] += nn(prob.astype(BF16), dm[qi, h, at, :])
                dkv[slot, hp, keys_at, 0:128] += nn(d_score, qm[qi, h, at, :])
                head_rows = pl.ds(s * HD, HD)
                dqt[qi, hp, head_rows, at] += nn(kt[slot, hp, head_rows, keys_at], d_score)

        over_parts(parts, tile)

    far = 1 - core
    ot[...] = jnp.zeros_like(ot)
    tot[...] = jnp.zeros_like(tot)
    split_heads(q, qm, 0)
    turn(OWN, 0)
    attend(0, 0, OWN, 0, LOWER, 0)
    for d in ways:
        kv_sends[1, d].wait_recv()
        forward(1, d)
    for d in ways:
        d_sends[d].wait_recv()
    df = send(do.at[0], do.at[1], s_f.at[0], r_f.at[0], (behind, x))
    turn(OWN, 1)
    attend(0, 0, OWN, 0, LOWER, 1)
    dqt[...] = jnp.zeros_like(dqt)
    dkv[...] = jnp.zeros_like(dkv)
    for d in range(nx):
        qf_sends[d].wait_recv()
    split_heads(q, qm, 1)
    of_sends = []
    for hp in (0, 1):
        for d in (0, 1, 3, 2):
            z_sends[hp, d].wait_recv()
            forward_pair(hp, d)
        turn(PREV, hp)
        attend(2, 1, PREV, 4, UPPER, hp)
        for d in range(nx):
            pp_sends[hp, d].wait_recv()
            sp_sends[hp, d].wait_recv()
        turn(PREVX, hp)
        turn(PAIR, hp)
        attend(4, far, PREVX + core, 3 - 2 * core, FULL, hp)
        of_s[hp] = ot[1, hp].astype(BF16)
        for s in (0, 1):
            for row in range(4):
                tf_s[hp, row * 2 + s : row * 2 + s + 1, :] = tot[1, hp * 2 + s]
        of_sends.append(
            (
                send(tf_s.at[hp], tf_r.at[hp], s_f.at[1 + hp], r_f.at[1 + hp], (ahead, x)),
                send(of_s.at[hp], of_r.at[hp], s_f.at[3 + hp], r_f.at[3 + hp], (ahead, x)),
            )
        )

        def near_blocks(j, carry):
            attend(1 + 2 * j, 0, PREV + j, 2 - j * (1 - 2 * core), FULL, hp)
            return carry

        lax.fori_loop(0, 2, near_blocks, 0)
    df.wait_recv()
    split_heads(do, dm, 0)
    split_heads(do, dm, 1)

    sent, cx_sends = [], {}
    for hp in (0, 1):
        for copy in of_sends[hp]:
            copy.wait_recv()
        d_turned = do[0, :, hp * 128 : hp * 128 + 128].astype(F32).T
        for s in (0, 1):
            head_rows = slice(s * HD, (s + 1) * HD)
            total = tot[0, hp * 2 + s] + tf_r[hp, s : s + 1, :]
            whole = ot[0, hp, head_rows, :] + of_r[hp, head_rows, :].astype(F32)
            context = (whole / total).astype(BF16).astype(F32)
            ctxt[head_rows, :] = context
            st_s[hp, s : s + 1, :] = 1.0 / total
            st_s[hp, 4 + s : 5 + s, :] = jnp.sum(d_turned[head_rows, :] * context, axis=0, keepdims=True)
        stat[0, hp] = st_s[hp]
        st = send(st_s.at[hp], stat.at[1, hp], s_f.at[5 + hp], r_f.at[5 + hp], (behind, x))
        lanes = pl.ds(hp * 128, 128)
        for d in (2, 1, 3, 0):
            block = ctxt[:, row_block(peer_at[d])].T.astype(BF16)
            if d:
                slot = hp * nx + d
                cxs[hp, d] = block
                cx_sends[hp, d] = send(
                    cxs.at[hp, d], cx.at[d, :, lanes], s_cx.at[slot], r_cx.at[slot], (c, peer_at[d])
                )
            else:
                cx[0, :, lanes] = block

        def near_grads(j, carry):
            grads(1 + 2 * j, 0, PREV + j, hp, FULL)
            return carry

        lax.fori_loop(0, 2, near_grads, 0)
        st.wait_recv()
        grads(4, far, PREVX + core, hp, FULL)
        pp_s[hp] = dkv[PREVX, hp].astype(BF16)
        ppg = send(pp_s.at[hp], pp_r.at[hp], s_gr.at[hp], r_gr.at[hp], (pair, x))
        sp_s[hp] = dkv[PAIR, hp].astype(BF16)
        spg = send(sp_s.at[hp], sp_r.at[hp], s_gr.at[2 + hp], r_gr.at[2 + hp], (pair, x))
        grads(2, 1, PREV, hp, UPPER)
        dqf_s[hp] = dqt[1, hp].astype(BF16)
        dqf = send(dqf_s.at[hp], dqf_r.at[hp], s_gr.at[6 + hp], r_gr.at[6 + hp], (ahead, x))
        ppg.wait_recv()
        ps_s[hp] = (dkv[PREV, hp] + pp_r[hp].astype(F32)).astype(BF16)
        psg = send(ps_s.at[hp], ps_r.at[hp], s_gr.at[4 + hp], r_gr.at[4 + hp], (behind, x))
        sent.append((spg, dqf, psg))
    for hp in (0, 1):
        grads(0, 0, OWN, hp, LOWER)

    g_sends = {}

    def give(group):
        if group == 1:
            for hp in (0, 1):
                sent[hp][1].wait_recv()
                dqt[0, hp] = (dqt[0, hp] + dqf_r[hp].astype(F32)) * scale
        else:
            hp = group // 2
            spg, _, psg = sent[hp]
            spg.wait_recv()
            psg.wait_recv()
        for d in (2, 1, 3, 0):
            at = row_block(peer_at[d])
            out = gs.at[group, d] if d else g.at[group, 0]
            if group == 1:
                for hp in (0, 1):
                    out[:, hp * 128 : hp * 128 + 128] = dqt[0, hp, :, at].T.astype(BF16)
            else:
                hp = group // 2
                total = dkv[OWN, hp, at, :] + ps_r[hp, at, :].astype(F32) + sp_r[hp, at, :].astype(F32)
                out[:, 0:128] = (total[:, 0:128] * scale).astype(BF16)
                out[:, 128:256] = total[:, 128:256].astype(BF16)
            if d:
                slot = group * nx + d
                g_sends[group, d] = send(
                    gs.at[group, d], g.at[group, d], s_g.at[slot], r_g.at[slot], (c, peer_at[d])
                )

    def take(group, d):
        if d:
            g_sends[group, d].wait_recv()
        if group == 1:
            return nt(g[1, d], w3[0, :, columns(source[d])])
        cols = pl.ds(pl.multiple_of(source[d] * width + (group // 2) * 128, 128), 128)
        return nt(g[group, d, :, 0:128], w3[1, :, cols]) + nt(g[group, d, :, 128:256], w3[2, :, cols])

    give(0)
    give(1)
    acc = nn(cx[0], wout[columns(x), :])
    for d in ways:
        for hp in (0, 1):
            cx_sends[hp, d].wait_recv()
        acc = acc + nn(cx[d], wout[columns(source[d]), :])
    att_out[...] = acc.astype(BF16)
    gacc[...] = take(0, 0) + take(1, 0)
    for d in ways:
        gacc[...] += take(0, d)
    give(2)
    for d in ways:
        gacc[...] += take(1, d)
    gacc[...] += take(2, 0)
    for d in ways:
        gacc[...] += take(2, d)
    gm[pl.ds(HALO, rows), :] = gacc[...].astype(BF16)
    convolve(gm, exchange_edges(gm, 2), ig_out, True)

    for copy in started:
        copy.wait_send()


def settle_kernel(a_hbm, b_hbm, a_out, b_out, held, sems):
    ins = [pltpu.make_async_copy(src, held.at[i], sems.at[i]) for i, src in enumerate((a_hbm, b_hbm))]
    outs = [pltpu.make_async_copy(held.at[i], dst, sems.at[2 + i]) for i, dst in enumerate((a_out, b_out))]
    for copy in ins:
        copy.start()
    for first, second in zip(ins, outs):
        first.wait()
        second.start()
    for copy in outs:
        copy.wait()


def on_device(tokens, conv_kernel, w_qkv, w_out, lengths, cotangent):
    rows, model = tokens.shape
    vmem = lambda shape, dtype: pltpu.VMEM(shape, dtype)
    dma = lambda count: pltpu.SemaphoreType.DMA((count,))
    scratch = [
        vmem((rows + 2 * HALO, model), BF16),
        vmem((rows + 2 * HALO, model), F32),
        vmem((KS, rows, 128), F32),
        vmem((rows, model), BF16),
        vmem((3, model, model), BF16),
        vmem((model, model), BF16),
        vmem((rows, model), BF16),
        vmem((4, 2, rows, 256), BF16),
        vmem((4, rows, 256), BF16),
        vmem((4, rows, 256), BF16),
        vmem((4, 2, 512, 256), BF16),
        vmem((2, 512, 256), BF16),
        vmem((2, 512, 256), BF16),
        vmem((4, 2, 128, 512), BF16),
        vmem((4, 2, 128, 512), BF16),
        vmem((2, 4, 512, 128), BF16),
        vmem((2, 4, 512, 128), BF16),
        vmem((2, 8, 512), I32),
        vmem((5, 4, 512, 512), F32),
        vmem((2, 2, 128, 512), F32),
        vmem((2, 4, 1, 512), F32),
        vmem((2, 128, 512), BF16),
        vmem((2, 128, 512), BF16),
        vmem((2, 8, 512), F32),
        vmem((2, 8, 512), F32),
        vmem((2, 2, 8, 512), F32),
        vmem((2, 8, 512), F32),
        vmem((128, 512), F32),
        vmem((2, 4, rows, 128), BF16),
        vmem((4, rows, 256), BF16),
        vmem((4, 2, 512, 256), F32),
        vmem((2, 2, 128, 512), F32),
        vmem((2, 512, 256), BF16),
        vmem((2, 512, 256), BF16),
        vmem((2, 512, 256), BF16),
        vmem((2, 512, 256), BF16),
        vmem((2, 512, 256), BF16),
        vmem((2, 512, 256), BF16),
        vmem((2, 128, 512), BF16),
        vmem((2, 128, 512), BF16),
        vmem((3, 4, rows, 256), BF16),
        vmem((3, 4, rows, 256), BF16),
        vmem((rows + 2 * HALO, model), BF16),
        vmem((rows, model), F32),
        vmem(conv_kernel.shape, F32),
        pltpu.SMEM(lengths.shape, I32),
        dma(8),
    ]
    for count in (4, 8, 8, 8, 8, 4, 4, 4, 7, 8, 8, 12):
        scratch += [dma(count), dma(count)]
    whole = pl.BlockSpec(memory_space=pltpu.VMEM)
    anywhere = pl.BlockSpec(memory_space=pl.ANY)
    out = jax.ShapeDtypeStruct((rows, model), BF16)
    attended, input_grad = pl.pallas_call(
        functools.partial(layer_kernel, lax.axis_size("ctx")),
        out_shape=(out, out),
        in_specs=[anywhere] * 6,
        out_specs=(whole, whole),
        scratch_shapes=scratch,
        compiler_params=pltpu.CompilerParams(
            collective_id=0, has_side_effects=True, vmem_limit_bytes=66_000_000
        ),
    )(tokens, cotangent, w_qkv, w_out, conv_kernel, lengths)
    return pl.pallas_call(
        settle_kernel,
        out_shape=(out, out),
        in_specs=[anywhere] * 2,
        out_specs=(anywhere, anywhere),
        scratch_shapes=[vmem((2, rows, model), BF16), dma(4)],
    )(attended, input_grad)


def solution(mesh):
    placed = (P(("ctx", "head"), None), P(), P(), P(), P(), P(("ctx", "head"), None))
    return jax.shard_map(
        on_device,
        mesh=mesh,
        in_specs=placed,
        out_specs=(P(("ctx", "head"), None), P(("ctx", "head"), None)),
        check_vma=False,
    )
```

```python
import functools
import math

import jax
import jax.numpy as jnp
from jax import lax
from jax.experimental import pallas as pl
from jax.experimental.pallas import tpu as pltpu
from jax.sharding import PartitionSpec as P

HD = 64
KS = 7
HALO = 16
OWN, PREV, PREVX, PAIR = 0, 1, 2, 3
MESH = pl.DeviceIdType.MESH
F32, BF16, I32 = jnp.float32, jnp.bfloat16, jnp.int32


def nt(a, b):
    return lax.dot_general(a, b, (((1,), (1,)), ((), ())), preferred_element_type=F32)


def nn(a, b):
    return jnp.dot(a, b, preferred_element_type=F32)


def layer_kernel(
    n_ctx,
    tok_hbm,
    cot_hbm,
    wqkv_hbm,
    wout_hbm,
    convk_hbm,
    lens_hbm,
    att_out,
    ig_out,
    ext,
    ext32,
    cmask,
    cot,
    w3,
    wout,
    mixed,
    kvs,
    qs,
    ds_,
    kv,
    q,
    do,
    kt,
    vt,
    qm,
    dm,
    starts,
    e_ref,
    ot,
    tot,
    of_s,
    of_r,
    tf_s,
    tf_r,
    stat,
    st_s,
    ctxt,
    cxs,
    cx,
    dkv,
    dqt,
    pp_s,
    pp_r,
    sp_s,
    sp_r,
    ps_s,
    ps_r,
    dqf_s,
    dqf_r,
    gs,
    g,
    gm,
    gacc,
    convk,
    lens,
    ld,
    s_h,
    r_h,
    s_kv,
    r_kv,
    s_z,
    r_z,
    s_sp,
    r_sp,
    s_pp,
    r_pp,
    s_q,
    r_q,
    s_d,
    r_d,
    s_qf,
    r_qf,
    s_f,
    r_f,
    s_cx,
    r_cx,
    s_gr,
    r_gr,
    s_g,
    r_g,
):
    c, x = lax.axis_index("ctx"), lax.axis_index("head")
    core = lax.rem(c, 2)
    ahead = lax.rem(c + 2, n_ctx)
    behind = lax.rem(c + n_ctx - 2, n_ctx)
    pair = c + 1 - 2 * core
    rows, width = 128, 256
    seq = 512
    nx = 4
    model = 1024

    up_x = lax.rem(x + 1, nx)
    up_c = lax.rem(c + (x + 1) // nx, n_ctx)
    dn_x = lax.rem(x + nx - 1, nx)
    dn_c = lax.rem(c + n_ctx - (nx - x) // nx, n_ctx)

    loads = [
        pltpu.make_async_copy(tok_hbm, ext.at[pl.ds(HALO, rows), :], ld.at[0]),
        pltpu.make_async_copy(lens_hbm, lens, ld.at[1]),
        pltpu.make_async_copy(convk_hbm, convk, ld.at[2]),
        pltpu.make_async_copy(wqkv_hbm.at[:, pl.ds(model, model)], w3.at[1], ld.at[3]),
        pltpu.make_async_copy(wqkv_hbm.at[:, pl.ds(2 * model, model)], w3.at[2], ld.at[4]),
        pltpu.make_async_copy(wqkv_hbm.at[:, pl.ds(0, model)], w3.at[0], ld.at[5]),
        pltpu.make_async_copy(cot_hbm, cot, ld.at[6]),
        pltpu.make_async_copy(wout_hbm, wout, ld.at[7]),
    ]
    barrier = pltpu.get_barrier_semaphore()
    peers = [(c, lax.rem(x + d, nx)) for d in (1, 2, 3)]
    peers += [(ahead, x), (behind, x), (pair, x), (up_c, up_x), (dn_c, dn_x)]
    for peer in peers:
        pl.semaphore_signal(barrier, inc=1, device_id=peer, device_id_type=MESH)
    for load in loads:
        load.start()
    loads[0].wait()
    pl.semaphore_wait(barrier, len(peers))

    started = []

    def send(src, dst, ss, rs, peer):
        copy = pltpu.make_async_remote_copy(
            src_ref=src, dst_ref=dst, send_sem=ss, recv_sem=rs, device_id=peer, device_id_type=MESH
        )
        copy.start()
        started.append(copy)
        return copy

    def exchange_edges(buf, base):
        up = send(
            buf.at[pl.ds(rows, HALO), :], buf.at[pl.ds(0, HALO), :],
            s_h.at[base], r_h.at[base], (up_c, up_x),
        )
        down = send(
            buf.at[pl.ds(HALO, HALO), :], buf.at[pl.ds(HALO + rows, HALO), :],
            s_h.at[base + 1], r_h.at[base + 1], (dn_c, dn_x),
        )
        return up, down

    edges = exchange_edges(ext, 0)

    loads[1].wait()
    ends = []
    run = jnp.int32(0)
    for i in range(lens.shape[0]):
        run = run + lens[i]
        ends.append(run)
    row_pos = (c * nx + x) * rows + lax.broadcasted_iota(I32, (rows, 128), 0)
    first = jnp.zeros((rows, 128), I32)
    for end in ends:
        first = jnp.where(row_pos >= end, end, first)
    last = jnp.zeros((rows, 128), I32)
    for end in reversed(ends):
        last = jnp.where(row_pos < end, end, last)
    for t in range(KS):
        near = row_pos + (t - KS // 2)
        cmask[t] = jnp.where((near >= first) & (near < last), 1.0, 0.0).astype(F32)

    def columns(p):
        return pl.ds(pl.multiple_of(p * width, width), width)

    def row_block(p):
        return pl.ds(pl.multiple_of(p * rows, rows), rows)

    peer_at = [lax.rem(x + d, nx) for d in range(nx)]
    source = [lax.rem(x + nx - d, nx) for d in range(nx)]
    mine = row_block(x)
    ways = (1, 3, 2)

    def convolve(buf, edges, out, flip):
        def part(at, count):
            def chunk(i, carry):
                lanes = pl.ds(pl.multiple_of(i * 128, 128), 128)
                acc = ext32[pl.ds(HALO + at, count), lanes]
                for t in range(KS):
                    tap = convk[pl.ds(KS - 1 - t if flip else t, 1), lanes]
                    near = ext32[pl.ds(HALO + at - KS // 2 + t, count), lanes]
                    acc = acc + tap * near * cmask[t, pl.ds(at, count), :]
                out[pl.ds(at, count), lanes] = acc.astype(BF16)
                return carry

            lax.fori_loop(0, model // 128, chunk, 0)

        inner = pl.ds(HALO, rows)
        ext32[inner, :] = buf[inner, :].astype(F32)
        part(HALO, rows - 2 * HALO)
        for edge in edges:
            edge.wait_recv()
        for side in (0, HALO + rows):
            ext32[pl.ds(side, HALO), :] = buf[pl.ds(side, HALO), :].astype(F32)
        part(0, HALO)
        part(rows - HALO, HALO)

    loads[2].wait()
    convolve(ext, edges, mixed, False)

    kv_sends, z_sends, sp_sends, pp_sends, q_sends, d_sends, qf_sends = {}, {}, {}, {}, {}, {}, {}

    def give_kv(hp, d):
        slot = hp * nx + d
        kv_sends[hp, d] = send(
            kvs.at[d, hp], kv.at[OWN, hp, mine, :], s_kv.at[slot], r_kv.at[slot], (c, peer_at[d])
        )

    def forward(hp, d):
        at, slot = row_block(source[d]), hp * nx + d
        block = kv.at[OWN, hp, at, :]
        z_sends[hp, d] = send(block, kv.at[PREV, hp, at, :], s_z.at[slot], r_z.at[slot], (ahead, x))
        sp_sends[hp, d] = send(block, kv.at[PAIR, hp, at, :], s_sp.at[slot], r_sp.at[slot], (pair, x))

    def forward_pair(hp, d):
        at, slot = row_block(source[d]), hp * nx + d
        pp_sends[hp, d] = send(
            kv.at[PREV, hp, at, :], kv.at[PREVX, hp, at, :], s_pp.at[slot], r_pp.at[slot], (pair, x)
        )

    def forward_q(hp, d):
        at, slot = row_block(source[d]), hp * nx + d
        qf_sends[hp, d] = send(
            q.at[0, hp, at, :], q.at[1, hp, at, :], s_qf.at[slot], r_qf.at[slot], (behind, x)
        )

    def give_q(hp, d):
        slot = hp * nx + d
        q_sends[hp, d] = send(
            qs.at[d, hp], q.at[0, hp, mine, :], s_q.at[slot], r_q.at[slot], (c, peer_at[d])
        )

    loads[3].wait()
    loads[4].wait()
    for d in (2, 1, 3, 0):
        for part in (0, 1):
            block = nn(mixed[...], w3[1 + part, :, columns(peer_at[d])]).astype(BF16)
            for hp in (0, 1):
                piece = block[:, hp * 128 : hp * 128 + 128]
                if d:
                    kvs[d, hp, :, part * 128 : part * 128 + 128] = piece
                else:
                    kv[OWN, hp, mine, part * 128 : part * 128 + 128] = piece
        if d:
            give_kv(0, d)
    forward(0, 0)
    loads[5].wait()
    for d in (2, 1, 3, 0):
        block = nn(mixed[...], w3[0, :, columns(peer_at[d])]).astype(BF16)
        for hp in (0, 1):
            piece = block[:, hp * 128 : hp * 128 + 128]
            if d:
                qs[d, hp] = piece
            else:
                q[0, hp, mine, :] = piece
        if d:
            give_q(0, d)
    forward_q(0, 0)
    for d in (2, 1, 3):
        give_kv(1, d)
    for d in (2, 1, 3):
        give_q(1, d)
    for d in ways:
        kv_sends[0, d].wait_recv()
        forward(0, d)
    forward(1, 0)
    forward_q(1, 0)

    loads[6].wait()
    loads[7].wait()
    for d in (2, 1, 3, 0):
        block = nt(cot[...], wout[columns(peer_at[d]), :]).astype(BF16)
        if d:
            ds_[d] = block
            d_sends[d] = send(ds_.at[d], do.at[0, mine, :], s_d.at[d], r_d.at[d], (c, peer_at[d]))
        else:
            do[0, mine, :] = block
    ot[...] = jnp.zeros_like(ot)
    tot[...] = jnp.zeros_like(tot)
    dqt[...] = jnp.zeros_like(dqt)
    dkv[...] = jnp.zeros_like(dkv)

    lane = lax.broadcasted_iota(I32, (8, seq), 1)
    for qi, shard in ((0, c), (1, ahead)):
        pos = shard * seq + lane
        first = jnp.zeros((8, seq), I32)
        for end in ends:
            first = jnp.where(pos >= end, end, first)
        starts[qi] = first
    half = lax.broadcasted_iota(I32, (seq, 128), 1) // HD
    for d in ways:
        q_sends[0, d].wait_recv()
        forward_q(0, d)

    def split_pair(block, dst, qi, hp):
        block = block.astype(F32)
        for s in (0, 1):
            dst[qi, hp * 2 + s] = jnp.where(half == s, block, 0.0).astype(BF16)

    def turn(slot, hp):
        kt[slot, hp] = kv[slot, hp, :, 0:128].astype(F32).T.astype(BF16)
        vt[slot, hp] = kv[slot, hp, :, 128:256].astype(F32).T.astype(BF16)

    scale = HD ** -0.5
    scale2 = scale * math.log2(math.e)
    kc = 256
    FULL = ((0, 0, seq), (kc, 0, seq))
    LOWER = ((0, 0, seq), (kc, kc, seq - kc))
    UPPER = ((0, 0, kc), (kc, 0, seq))

    def over_parts(parts, tile):
        if parts is FULL:

            def step(part, carry):
                tile(pl.multiple_of(part * kc, kc), 0, seq)
                return carry

            lax.fori_loop(0, seq // kc, step, 0)
        else:
            for part in parts:
                tile(*part)

    def attend(block, qi, slot, distance, parts, hp):
        base = (jnp.where(qi == 0, c, ahead) - distance) * seq

        def tile(k0, q0, queries):
            at = pl.ds(q0, queries)
            keys = kv[slot, hp, pl.ds(k0, kc), 0:128]
            k_iota = lax.broadcasted_iota(I32, (kc, queries), 0)
            ok = base + k0 + k_iota >= starts[qi, 0:1, at]
            if parts is LOWER:
                q_iota = lax.broadcasted_iota(I32, (kc, queries), 1)
                ok = ok & (k0 + k_iota <= q0 + q_iota)
            for s in (0, 1):
                h = hp * 2 + s
                score = nt(keys, qm[qi, h, at, :])
                e = jnp.where(ok, jnp.exp2(score * scale2), 0.0)
                e_ref[block, h, pl.ds(k0, kc), at] = e
                tot[qi, h, :, at] += jnp.sum(e, axis=0, keepdims=True)
                head_rows = pl.ds(s * HD, HD)
                ot[qi, hp, head_rows, at] += nn(vt[slot, hp, head_rows, pl.ds(k0, kc)], e.astype(BF16))

        over_parts(parts, tile)

    def grads(block, qi, slot, hp, k0, q0, queries):
        at = pl.ds(q0, queries)
        keys_at = pl.ds(k0, kc)
        values = kv[slot, hp, keys_at, 128:256]
        for s in (0, 1):
            h = hp * 2 + s
            prob = e_ref[block, h, keys_at, at] * stat[qi, hp, s : s + 1, at]
            d_prob = nt(values, dm[qi, h, at, :])
            d_score = (prob * (d_prob - stat[qi, hp, 4 + s : 5 + s, at])).astype(BF16)
            dkv[slot, hp, keys_at, 128:256] += nn(prob.astype(BF16), dm[qi, h, at, :])
            dkv[slot, hp, keys_at, 0:128] += nn(d_score, qm[qi, h, at, :])
            head_rows = pl.ds(s * HD, HD)
            dqt[qi, hp, head_rows, at] += nn(kt[slot, hp, head_rows, keys_at], d_score)

    far = 1 - core
    def pass_pair(hp):
        for d in (0, 1, 3, 2):
            z_sends[hp, d].wait_recv()
            forward_pair(hp, d)

    def pass_on(d):
        kv_sends[1, d].wait_recv()
        forward(1, d)
        q_sends[1, d].wait_recv()
        forward_q(1, d)

    of_sends = []
    for hp in (0, 1):
        split_pair(q[0, hp], qm, 0, hp)
        turn(OWN, hp)
        attend(0, 0, OWN, 0, LOWER, hp)
        if hp == 1:
            for d in ways:
                d_sends[d].wait_recv()
            df = send(do.at[0], do.at[1], s_f.at[0], r_f.at[0], (behind, x))
        pass_pair(hp)
        for d in range(nx):
            qf_sends[hp, d].wait_recv()
        split_pair(q[1, hp], qm, 1, hp)
        turn(PREV, hp)
        attend(2, 1, PREV, 4, UPPER, hp)
        if hp == 0:
            pass_on(1)
            pass_on(3)
        attend(1, 0, PREV, 2, FULL, hp)
        if hp == 0:
            pass_on(2)
        for d in range(nx):
            pp_sends[hp, d].wait_recv()
            sp_sends[hp, d].wait_recv()
        turn(PREVX, hp)
        turn(PAIR, hp)

        def crossed(j, carry):
            distance = jnp.where(j == 0, 3 - 2 * core, 1 + 2 * core)
            attend(4 - j, (1 - j) * far, PREVX + (1 - j) * core, distance, FULL, hp)
            return carry

        lax.fori_loop(0, 2, crossed, 0)
        of_s[hp] = ot[1, hp].astype(BF16)
        for s in (0, 1):
            for row in range(4):
                tf_s[hp, row * 2 + s : row * 2 + s + 1, :] = tot[1, hp * 2 + s]
        of_sends.append(
            (
                send(tf_s.at[hp], tf_r.at[hp], s_f.at[1 + hp], r_f.at[1 + hp], (ahead, x)),
                send(of_s.at[hp], of_r.at[hp], s_f.at[3 + hp], r_f.at[3 + hp], (ahead, x)),
            )
        )
    df.wait_recv()
    for qi in (0, 1):
        for hp in (0, 1):
            split_pair(do[qi, :, hp * 128 : hp * 128 + 128], dm, qi, hp)

    g_sends = {}
    sent = [[], []]
    dqf_sends = [None, None]
    waiting = []

    def pass_back():
        while waiting:
            hp, part, ppg = waiting.pop()
            keys_at = pl.ds(part * kc, kc)
            slot = 8 + hp * 2 + part
            ppg.wait_recv()
            ps_s[hp, keys_at, :] = (dkv[PREV, hp, keys_at, :] + pp_r[hp, keys_at, :].astype(F32)).astype(BF16)
            sent[hp].append(
                send(
                    ps_s.at[hp, keys_at, :], ps_r.at[hp, keys_at, :], s_gr.at[slot], r_gr.at[slot], (behind, x)
                )
            )

    def give(group):
        if group == 1:
            for hp in (0, 1):
                dqf_sends[hp].wait_recv()
                dqt[0, hp] = (dqt[0, hp] + dqf_r[hp].astype(F32)) * scale
        else:
            hp = group // 2
            for copy in sent[hp]:
                copy.wait_recv()
        for d in (2, 1, 3, 0):
            at = row_block(peer_at[d])
            out = gs.at[group, d] if d else g.at[group, 0]
            if group == 1:
                for hp in (0, 1):
                    out[:, hp * 128 : hp * 128 + 128] = dqt[0, hp, :, at].T.astype(BF16)
            else:
                hp = group // 2
                total = dkv[OWN, hp, at, :] + ps_r[hp, at, :].astype(F32) + sp_r[hp, at, :].astype(F32)
                out[:, 0:128] = (total[:, 0:128] * scale).astype(BF16)
                out[:, 128:256] = total[:, 128:256].astype(BF16)
            if d:
                slot = group * nx + d
                g_sends[group, d] = send(
                    gs.at[group, d], g.at[group, d], s_g.at[slot], r_g.at[slot], (c, peer_at[d])
                )

    cx_sends = {}
    for hp in (0, 1):
        for copy in of_sends[hp]:
            copy.wait_recv()
        d_turned = do[0, :, hp * 128 : hp * 128 + 128].astype(F32).T
        for s in (0, 1):
            head_rows = slice(s * HD, (s + 1) * HD)
            total = tot[0, hp * 2 + s] + tf_r[hp, s : s + 1, :]
            whole = ot[0, hp, head_rows, :] + of_r[hp, head_rows, :].astype(F32)
            context = (whole / total).astype(BF16).astype(F32)
            ctxt[head_rows, :] = context
            st_s[hp, s : s + 1, :] = 1.0 / total
            st_s[hp, 4 + s : 5 + s, :] = jnp.sum(d_turned[head_rows, :] * context, axis=0, keepdims=True)
        stat[0, hp] = st_s[hp]
        st = send(st_s.at[hp], stat.at[1, hp], s_f.at[5 + hp], r_f.at[5 + hp], (behind, x))
        lanes = pl.ds(hp * 128, 128)
        for d in (2, 1, 3, 0):
            block = ctxt[:, row_block(peer_at[d])].T.astype(BF16)
            if d:
                slot = hp * nx + d
                cxs[hp, d] = block
                cx_sends[hp, d] = send(
                    cxs.at[hp, d], cx.at[d, :, lanes], s_cx.at[slot], r_cx.at[slot], (c, peer_at[d])
                )
            else:
                cx[0, :, lanes] = block

        for part in (0, 1):
            k0 = part * kc
            keys_at = pl.ds(k0, kc)
            slot = hp * 2 + part

            def near_grads(j, carry):
                grads(1 + 2 * j, 0, PREV + j, hp, k0, 0, seq)
                return carry

            lax.fori_loop(0, 2, near_grads, 0)
            pass_back()
            if part == 0:
                st.wait_recv()
            grads(4, far, PREVX + core, hp, k0, 0, seq)
            pp_s[hp, keys_at, :] = dkv[PREVX, hp, keys_at, :].astype(BF16)
            ppg = send(
                pp_s.at[hp, keys_at, :], pp_r.at[hp, keys_at, :], s_gr.at[slot], r_gr.at[slot], (pair, x)
            )
            sp_s[hp, keys_at, :] = dkv[PAIR, hp, keys_at, :].astype(BF16)
            sent[hp].append(
                send(
                    sp_s.at[hp, keys_at, :], sp_r.at[hp, keys_at, :],
                    s_gr.at[4 + slot], r_gr.at[4 + slot], (pair, x),
                )
            )
            grads(2, 1, PREV, hp, *UPPER[part])
            waiting.append((hp, part, ppg))
            if part == 1:
                dqf_s[hp] = dqt[1, hp].astype(BF16)
                dqf_sends[hp] = send(
                    dqf_s.at[hp], dqf_r.at[hp], s_gr.at[12 + hp], r_gr.at[12 + hp], (ahead, x)
                )
                if hp == 1:
                    give(0)
                grads(0, 0, OWN, hp, *LOWER[1])
                pass_back()
                grads(0, 0, OWN, hp, *LOWER[0])
    give(1)

    def take(group, d):
        if d:
            g_sends[group, d].wait_recv()
        if group == 1:
            return nt(g[1, d], w3[0, :, columns(source[d])])
        cols = pl.ds(pl.multiple_of(source[d] * width + (group // 2) * 128, 128), 128)
        return nt(g[group, d, :, 0:128], w3[1, :, cols]) + nt(g[group, d, :, 128:256], w3[2, :, cols])

    acc = nn(cx[0], wout[columns(x), :])
    for d in ways:
        for hp in (0, 1):
            cx_sends[hp, d].wait_recv()
        acc = acc + nn(cx[d], wout[columns(source[d]), :])
    att_out[...] = acc.astype(BF16)
    gacc[...] = take(0, 0) + take(1, 0)
    for d in ways:
        gacc[...] += take(0, d)
    give(2)
    for d in ways:
        gacc[...] += take(1, d)
    gacc[...] += take(2, 0)
    for d in ways:
        gacc[...] += take(2, d)
    gm[pl.ds(HALO, rows), :] = gacc[...].astype(BF16)
    convolve(gm, exchange_edges(gm, 2), ig_out, True)

    for copy in started:
        copy.wait_send()


def settle_kernel(a_hbm, b_hbm, a_out, b_out, held, sems):
    ins = [pltpu.make_async_copy(src, held.at[i], sems.at[i]) for i, src in enumerate((a_hbm, b_hbm))]
    outs = [pltpu.make_async_copy(held.at[i], dst, sems.at[2 + i]) for i, dst in enumerate((a_out, b_out))]
    for copy in ins:
        copy.start()
    for first, second in zip(ins, outs):
        first.wait()
        second.start()
    for copy in outs:
        copy.wait()


def on_device(tokens, conv_kernel, w_qkv, w_out, lengths, cotangent):
    rows, model = tokens.shape
    vmem = lambda shape, dtype: pltpu.VMEM(shape, dtype)
    dma = lambda count: pltpu.SemaphoreType.DMA((count,))
    scratch = [
        vmem((rows + 2 * HALO, model), BF16),
        vmem((rows + 2 * HALO, model), F32),
        vmem((KS, rows, 128), F32),
        vmem((rows, model), BF16),
        vmem((3, model, model), BF16),
        vmem((model, model), BF16),
        vmem((rows, model), BF16),
        vmem((4, 2, rows, 256), BF16),
        vmem((4, 2, rows, 128), BF16),
        vmem((4, rows, 256), BF16),
        vmem((4, 2, 512, 256), BF16),
        vmem((2, 2, 512, 128), BF16),
        vmem((2, 512, 256), BF16),
        vmem((4, 2, 128, 512), BF16),
        vmem((4, 2, 128, 512), BF16),
        vmem((2, 4, 512, 128), BF16),
        vmem((2, 4, 512, 128), BF16),
        vmem((2, 8, 512), I32),
        vmem((5, 4, 512, 512), F32),
        vmem((2, 2, 128, 512), F32),
        vmem((2, 4, 1, 512), F32),
        vmem((2, 128, 512), BF16),
        vmem((2, 128, 512), BF16),
        vmem((2, 8, 512), F32),
        vmem((2, 8, 512), F32),
        vmem((2, 2, 8, 512), F32),
        vmem((2, 8, 512), F32),
        vmem((128, 512), F32),
        vmem((2, 4, rows, 128), BF16),
        vmem((4, rows, 256), BF16),
        vmem((4, 2, 512, 256), F32),
        vmem((2, 2, 128, 512), F32),
        vmem((2, 512, 256), BF16),
        vmem((2, 512, 256), BF16),
        vmem((2, 512, 256), BF16),
        vmem((2, 512, 256), BF16),
        vmem((2, 512, 256), BF16),
        vmem((2, 512, 256), BF16),
        vmem((2, 128, 512), BF16),
        vmem((2, 128, 512), BF16),
        vmem((3, 4, rows, 256), BF16),
        vmem((3, 4, rows, 256), BF16),
        vmem((rows + 2 * HALO, model), BF16),
        vmem((rows, model), F32),
        vmem(conv_kernel.shape, F32),
        pltpu.SMEM(lengths.shape, I32),
        dma(8),
    ]
    for count in (4, 8, 8, 8, 8, 8, 4, 8, 7, 8, 14, 12):
        scratch += [dma(count), dma(count)]
    whole = pl.BlockSpec(memory_space=pltpu.VMEM)
    anywhere = pl.BlockSpec(memory_space=pl.ANY)
    out = jax.ShapeDtypeStruct((rows, model), BF16)
    attended, input_grad = pl.pallas_call(
        functools.partial(layer_kernel, lax.axis_size("ctx")),
        out_shape=(out, out),
        in_specs=[anywhere] * 6,
        out_specs=(whole, whole),
        scratch_shapes=scratch,
        compiler_params=pltpu.CompilerParams(
            collective_id=0, has_side_effects=True, vmem_limit_bytes=66_000_000
        ),
    )(tokens, cotangent, w_qkv, w_out, conv_kernel, lengths)
    return pl.pallas_call(
        settle_kernel,
        out_shape=(out, out),
        in_specs=[anywhere] * 2,
        out_specs=(anywhere, anywhere),
        scratch_shapes=[vmem((2, rows, model), BF16), dma(4)],
    )(attended, input_grad)


def solution(mesh):
    placed = (P(("ctx", "head"), None), P(), P(), P(), P(), P(("ctx", "head"), None))
    return jax.shard_map(
        on_device,
        mesh=mesh,
        in_specs=placed,
        out_specs=(P(("ctx", "head"), None), P(("ctx", "head"), None)),
        check_vma=False,
    )
```

```python
import functools
import math

import jax
import jax.numpy as jnp
from jax import lax
from jax.experimental import pallas as pl
from jax.experimental.pallas import tpu as pltpu
from jax.sharding import PartitionSpec as P

HD = 64
KS = 7
HALO = 16
OWN, PREV, PREVX, PAIR = 0, 1, 2, 3
MESH = pl.DeviceIdType.MESH
F32, BF16, I32 = jnp.float32, jnp.bfloat16, jnp.int32


def nt(a, b):
    return lax.dot_general(a, b, (((1,), (1,)), ((), ())), preferred_element_type=F32)


def nn(a, b):
    return jnp.dot(a, b, preferred_element_type=F32)


def layer_kernel(
    n_ctx,
    tok_hbm,
    cot_hbm,
    wqkv_hbm,
    wout_hbm,
    convk_hbm,
    lens_hbm,
    att_out,
    ig_out,
    ext,
    ext32,
    cmask,
    cot,
    w3,
    wout,
    mixed,
    kvs,
    qs,
    ds_,
    kv,
    q,
    do,
    kt,
    vt,
    qm,
    dm,
    starts,
    e_ref,
    ot,
    tot,
    of_s,
    of_r,
    tf_s,
    tf_r,
    stat,
    st_s,
    ctxt,
    cxs,
    cx,
    dkv,
    dqt,
    pp_s,
    pp_r,
    sp_s,
    sp_r,
    ps_s,
    ps_r,
    dqf_s,
    dqf_r,
    gs,
    g,
    gm,
    gacc,
    convk,
    lens,
    ld,
    s_h,
    r_h,
    s_kv,
    r_kv,
    s_z,
    r_z,
    s_sp,
    r_sp,
    s_pp,
    r_pp,
    s_q,
    r_q,
    s_d,
    r_d,
    s_qf,
    r_qf,
    s_f,
    r_f,
    s_cx,
    r_cx,
    s_gr,
    r_gr,
    s_g,
    r_g,
):
    c, x = lax.axis_index("ctx"), lax.axis_index("head")
    core = lax.rem(c, 2)
    ahead = lax.rem(c + 2, n_ctx)
    behind = lax.rem(c + n_ctx - 2, n_ctx)
    pair = c + 1 - 2 * core
    rows, width = 128, 256
    seq = 512
    nx = 4
    model = 1024

    up_x = lax.rem(x + 1, nx)
    up_c = lax.rem(c + (x + 1) // nx, n_ctx)
    dn_x = lax.rem(x + nx - 1, nx)
    dn_c = lax.rem(c + n_ctx - (nx - x) // nx, n_ctx)

    loads = [
        pltpu.make_async_copy(tok_hbm, ext.at[pl.ds(HALO, rows), :], ld.at[0]),
        pltpu.make_async_copy(lens_hbm, lens, ld.at[1]),
        pltpu.make_async_copy(convk_hbm, convk, ld.at[2]),
        pltpu.make_async_copy(wqkv_hbm.at[:, pl.ds(model, model)], w3.at[1], ld.at[3]),
        pltpu.make_async_copy(wqkv_hbm.at[:, pl.ds(2 * model, model)], w3.at[2], ld.at[4]),
        pltpu.make_async_copy(wqkv_hbm.at[:, pl.ds(0, model)], w3.at[0], ld.at[5]),
        pltpu.make_async_copy(cot_hbm, cot, ld.at[6]),
        pltpu.make_async_copy(wout_hbm, wout, ld.at[7]),
    ]
    barrier = pltpu.get_barrier_semaphore()
    peers = [(c, lax.rem(x + d, nx)) for d in (1, 2, 3)]
    peers += [(ahead, x), (behind, x), (pair, x), (up_c, up_x), (dn_c, dn_x)]
    for peer in peers:
        pl.semaphore_signal(barrier, inc=1, device_id=peer, device_id_type=MESH)
    for load in loads:
        load.start()
    loads[0].wait()
    pl.semaphore_wait(barrier, len(peers))

    started = []

    def send(src, dst, ss, rs, peer):
        copy = pltpu.make_async_remote_copy(
            src_ref=src, dst_ref=dst, send_sem=ss, recv_sem=rs, device_id=peer, device_id_type=MESH
        )
        copy.start()
        started.append(copy)
        return copy

    def exchange_edges(buf, base):
        up = send(
            buf.at[pl.ds(rows, HALO), :], buf.at[pl.ds(0, HALO), :],
            s_h.at[base], r_h.at[base], (up_c, up_x),
        )
        down = send(
            buf.at[pl.ds(HALO, HALO), :], buf.at[pl.ds(HALO + rows, HALO), :],
            s_h.at[base + 1], r_h.at[base + 1], (dn_c, dn_x),
        )
        return up, down

    edges = exchange_edges(ext, 0)

    loads[1].wait()
    ends = []
    run = jnp.int32(0)
    for i in range(lens.shape[0]):
        run = run + lens[i]
        ends.append(run)
    row_pos = (c * nx + x) * rows + lax.broadcasted_iota(I32, (rows, 128), 0)
    first = jnp.zeros((rows, 128), I32)
    for end in ends:
        first = jnp.where(row_pos >= end, end, first)
    last = jnp.zeros((rows, 128), I32)
    for end in reversed(ends):
        last = jnp.where(row_pos < end, end, last)
    for t in range(KS):
        near = row_pos + (t - KS // 2)
        cmask[t] = jnp.where((near >= first) & (near < last), 1.0, 0.0).astype(F32)

    def columns(p):
        return pl.ds(pl.multiple_of(p * width, width), width)

    def row_block(p):
        return pl.ds(pl.multiple_of(p * rows, rows), rows)

    peer_at = [lax.rem(x + d, nx) for d in range(nx)]
    source = [lax.rem(x + nx - d, nx) for d in range(nx)]
    mine = row_block(x)
    ways = (1, 3, 2)

    def convolve(buf, edges, out, flip):
        def part(at, count):
            def chunk(i, carry):
                lanes = pl.ds(pl.multiple_of(i * 128, 128), 128)
                acc = ext32[pl.ds(HALO + at, count), lanes]
                for t in range(KS):
                    tap = convk[pl.ds(KS - 1 - t if flip else t, 1), lanes]
                    near = ext32[pl.ds(HALO + at - KS // 2 + t, count), lanes]
                    acc = acc + tap * near * cmask[t, pl.ds(at, count), :]
                out[pl.ds(at, count), lanes] = acc.astype(BF16)
                return carry

            lax.fori_loop(0, model // 128, chunk, 0)

        inner = pl.ds(HALO, rows)
        ext32[inner, :] = buf[inner, :].astype(F32)
        part(HALO, rows - 2 * HALO)
        for edge in edges:
            edge.wait_recv()
        for side in (0, HALO + rows):
            ext32[pl.ds(side, HALO), :] = buf[pl.ds(side, HALO), :].astype(F32)
        part(0, HALO)
        part(rows - HALO, HALO)

    loads[2].wait()
    convolve(ext, edges, mixed, False)

    kv_sends, z_sends, sp_sends, pp_sends, q_sends, d_sends, qf_sends = {}, {}, {}, {}, {}, {}, {}

    def give_kv(hp, d):
        slot = hp * nx + d
        kv_sends[hp, d] = send(
            kvs.at[d, hp], kv.at[OWN, hp, mine, :], s_kv.at[slot], r_kv.at[slot], (c, peer_at[d])
        )

    def forward(hp, d):
        at, slot = row_block(source[d]), hp * nx + d
        block = kv.at[OWN, hp, at, :]
        z_sends[hp, d] = send(block, kv.at[PREV, hp, at, :], s_z.at[slot], r_z.at[slot], (ahead, x))
        sp_sends[hp, d] = send(block, kv.at[PAIR, hp, at, :], s_sp.at[slot], r_sp.at[slot], (pair, x))

    def forward_pair(hp, d):
        at, slot = row_block(source[d]), hp * nx + d
        pp_sends[hp, d] = send(
            kv.at[PREV, hp, at, :], kv.at[PREVX, hp, at, :], s_pp.at[slot], r_pp.at[slot], (pair, x)
        )

    def forward_q(hp, d):
        at, slot = row_block(source[d]), hp * nx + d
        qf_sends[hp, d] = send(
            q.at[0, hp, at, :], q.at[1, hp, at, :], s_qf.at[slot], r_qf.at[slot], (behind, x)
        )

    def give_q(hp, d):
        slot = hp * nx + d
        q_sends[hp, d] = send(
            qs.at[d, hp], q.at[0, hp, mine, :], s_q.at[slot], r_q.at[slot], (c, peer_at[d])
        )

    loads[3].wait()
    loads[4].wait()
    for d in (2, 1, 3, 0):
        for part in (0, 1):
            block = nn(mixed[...], w3[1 + part, :, columns(peer_at[d])]).astype(BF16)
            for hp in (0, 1):
                piece = block[:, hp * 128 : hp * 128 + 128]
                if d:
                    kvs[d, hp, :, part * 128 : part * 128 + 128] = piece
                else:
                    kv[OWN, hp, mine, part * 128 : part * 128 + 128] = piece
        if d:
            give_kv(0, d)
    forward(0, 0)
    loads[5].wait()
    for d in (2, 1, 3, 0):
        block = nn(mixed[...], w3[0, :, columns(peer_at[d])]).astype(BF16)
        for hp in (0, 1):
            piece = block[:, hp * 128 : hp * 128 + 128]
            if d:
                qs[d, hp] = piece
            else:
                q[0, hp, mine, :] = piece
        if d:
            give_q(0, d)
    forward_q(0, 0)

    loads[6].wait()
    loads[7].wait()
    for d in (2, 1, 3, 0):
        block = nt(cot[...], wout[columns(peer_at[d]), :]).astype(BF16)
        if d:
            ds_[d] = block
        else:
            do[0, mine, :] = block
    for d in ways:
        kv_sends[0, d].wait_recv()
        forward(0, d)
    ot[...] = jnp.zeros_like(ot)
    tot[...] = jnp.zeros_like(tot)
    dqt[...] = jnp.zeros_like(dqt)
    dkv[...] = jnp.zeros_like(dkv)
    lane = lax.broadcasted_iota(I32, (8, seq), 1)
    for qi, shard in ((0, c), (1, ahead)):
        pos = shard * seq + lane
        first = jnp.zeros((8, seq), I32)
        for end in ends:
            first = jnp.where(pos >= end, end, first)
        starts[qi] = first
    half = lax.broadcasted_iota(I32, (seq, 128), 1) // HD
    for d in ways:
        q_sends[0, d].wait_recv()
        forward_q(0, d)
    for d in (2, 1, 3):
        give_kv(1, d)
    forward(1, 0)
    for d in (2, 1, 3):
        give_q(1, d)
    forward_q(1, 0)
    for d in (2, 1, 3):
        d_sends[d] = send(ds_.at[d], do.at[0, mine, :], s_d.at[d], r_d.at[d], (c, peer_at[d]))

    def split_pair(block, dst, qi, hp):
        block = block.astype(F32)
        for s in (0, 1):
            dst[qi, hp * 2 + s] = jnp.where(half == s, block, 0.0).astype(BF16)

    def turn(slot, hp):
        kt[slot, hp] = kv[slot, hp, :, 0:128].astype(F32).T.astype(BF16)
        vt[slot, hp] = kv[slot, hp, :, 128:256].astype(F32).T.astype(BF16)

    scale = HD ** -0.5
    scale2 = scale * math.log2(math.e)
    kc = 256
    FULL = ((0, 0, seq), (kc, 0, seq))
    LOWER = ((0, 0, seq), (kc, kc, seq - kc))
    UPPER = ((0, 0, kc), (kc, 0, seq))

    def over_parts(parts, tile):
        if parts is FULL:

            def step(part, carry):
                tile(pl.multiple_of(part * kc, kc), 0, seq)
                return carry

            lax.fori_loop(0, seq // kc, step, 0)
        else:
            for part in parts:
                tile(*part)

    def attend(block, qi, slot, distance, parts, hp):
        base = (jnp.where(qi == 0, c, ahead) - distance) * seq

        def tile(k0, q0, queries):
            at = pl.ds(q0, queries)
            keys = kv[slot, hp, pl.ds(k0, kc), 0:128]
            k_iota = lax.broadcasted_iota(I32, (kc, queries), 0)
            ok = base + k0 + k_iota >= starts[qi, 0:1, at]
            if parts is LOWER:
                q_iota = lax.broadcasted_iota(I32, (kc, queries), 1)
                ok = ok & (k0 + k_iota <= q0 + q_iota)
            for s in (0, 1):
                h = hp * 2 + s
                score = nt(keys, qm[qi, h, at, :])
                e = jnp.where(ok, jnp.exp2(score * scale2), 0.0)
                e_ref[block, h, pl.ds(k0, kc), at] = e
                tot[qi, h, :, at] += jnp.sum(e, axis=0, keepdims=True)
                head_rows = pl.ds(s * HD, HD)
                ot[qi, hp, head_rows, at] += nn(vt[slot, hp, head_rows, pl.ds(k0, kc)], e.astype(BF16))

        over_parts(parts, tile)

    def grads(block, qi, slot, hp, k0, q0, queries):
        at = pl.ds(q0, queries)
        keys_at = pl.ds(k0, kc)
        values = kv[slot, hp, keys_at, 128:256]
        for s in (0, 1):
            h = hp * 2 + s
            prob = e_ref[block, h, keys_at, at] * stat[qi, hp, s : s + 1, at]
            d_prob = nt(values, dm[qi, h, at, :])
            d_score = (prob * (d_prob - stat[qi, hp, 4 + s : 5 + s, at])).astype(BF16)
            dkv[slot, hp, keys_at, 128:256] += nn(prob.astype(BF16), dm[qi, h, at, :])
            dkv[slot, hp, keys_at, 0:128] += nn(d_score, qm[qi, h, at, :])
            head_rows = pl.ds(s * HD, HD)
            dqt[qi, hp, head_rows, at] += nn(kt[slot, hp, head_rows, keys_at], d_score)

    far = 1 - core
    def pass_pair(hp):
        for d in (0, 1, 3, 2):
            z_sends[hp, d].wait_recv()
            forward_pair(hp, d)

    def pass_on(d):
        kv_sends[1, d].wait_recv()
        forward(1, d)
        q_sends[1, d].wait_recv()
        forward_q(1, d)

    of_sends = []
    for hp in (0, 1):
        split_pair(q[0, hp], qm, 0, hp)
        turn(OWN, hp)
        attend(0, 0, OWN, 0, LOWER, hp)
        if hp == 1:
            for d in ways:
                d_sends[d].wait_recv()
            df = send(do.at[0], do.at[1], s_f.at[0], r_f.at[0], (behind, x))
        pass_pair(hp)
        for d in range(nx):
            qf_sends[hp, d].wait_recv()
        split_pair(q[1, hp], qm, 1, hp)
        turn(PREV, hp)
        attend(2, 1, PREV, 4, UPPER, hp)
        if hp == 0:
            pass_on(1)
            pass_on(3)
        attend(1, 0, PREV, 2, FULL, hp)
        if hp == 0:
            pass_on(2)
        for d in range(nx):
            pp_sends[hp, d].wait_recv()
            sp_sends[hp, d].wait_recv()
        turn(PREVX, hp)
        turn(PAIR, hp)

        def crossed(j, carry):
            distance = jnp.where(j == 0, 3 - 2 * core, 1 + 2 * core)
            attend(4 - j, (1 - j) * far, PREVX + (1 - j) * core, distance, FULL, hp)
            return carry

        lax.fori_loop(0, 2, crossed, 0)
        of_s[hp] = ot[1, hp].astype(BF16)
        for s in (0, 1):
            for row in range(4):
                tf_s[hp, row * 2 + s : row * 2 + s + 1, :] = tot[1, hp * 2 + s]
        of_sends.append(
            (
                send(tf_s.at[hp], tf_r.at[hp], s_f.at[1 + hp], r_f.at[1 + hp], (ahead, x)),
                send(of_s.at[hp], of_r.at[hp], s_f.at[3 + hp], r_f.at[3 + hp], (ahead, x)),
            )
        )
    df.wait_recv()
    for qi in (0, 1):
        for hp in (0, 1):
            split_pair(do[qi, :, hp * 128 : hp * 128 + 128], dm, qi, hp)

    g_sends = {}
    sent = [[], []]
    dqf_sends = [None, None]
    waiting = []

    def pass_back():
        while waiting:
            hp, part, ppg = waiting.pop()
            keys_at = pl.ds(part * kc, kc)
            slot = 8 + hp * 2 + part
            ppg.wait_recv()
            ps_s[hp, keys_at, :] = (dkv[PREV, hp, keys_at, :] + pp_r[hp, keys_at, :].astype(F32)).astype(BF16)
            sent[hp].append(
                send(
                    ps_s.at[hp, keys_at, :], ps_r.at[hp, keys_at, :], s_gr.at[slot], r_gr.at[slot], (behind, x)
                )
            )

    def give(group):
        if group == 1:
            for hp in (0, 1):
                dqf_sends[hp].wait_recv()
                dqt[0, hp] = (dqt[0, hp] + dqf_r[hp].astype(F32)) * scale
        else:
            hp = group // 2
            for copy in sent[hp]:
                copy.wait_recv()
        for d in (2, 1, 3, 0):
            at = row_block(peer_at[d])
            out = gs.at[group, d] if d else g.at[group, 0]
            if group == 1:
                for hp in (0, 1):
                    out[:, hp * 128 : hp * 128 + 128] = dqt[0, hp, :, at].T.astype(BF16)
            else:
                hp = group // 2
                total = dkv[OWN, hp, at, :] + ps_r[hp, at, :].astype(F32) + sp_r[hp, at, :].astype(F32)
                out[:, 0:128] = (total[:, 0:128] * scale).astype(BF16)
                out[:, 128:256] = total[:, 128:256].astype(BF16)
            if d:
                slot = group * nx + d
                g_sends[group, d] = send(
                    gs.at[group, d], g.at[group, d], s_g.at[slot], r_g.at[slot], (c, peer_at[d])
                )

    cx_sends = {}
    for hp in (0, 1):
        for copy in of_sends[hp]:
            copy.wait_recv()
        d_turned = do[0, :, hp * 128 : hp * 128 + 128].astype(F32).T
        for s in (0, 1):
            head_rows = slice(s * HD, (s + 1) * HD)
            total = tot[0, hp * 2 + s] + tf_r[hp, s : s + 1, :]
            whole = ot[0, hp, head_rows, :] + of_r[hp, head_rows, :].astype(F32)
            context = (whole / total).astype(BF16).astype(F32)
            ctxt[head_rows, :] = context
            st_s[hp, s : s + 1, :] = 1.0 / total
            st_s[hp, 4 + s : 5 + s, :] = jnp.sum(d_turned[head_rows, :] * context, axis=0, keepdims=True)
        stat[0, hp] = st_s[hp]
        st = send(st_s.at[hp], stat.at[1, hp], s_f.at[5 + hp], r_f.at[5 + hp], (behind, x))
        lanes = pl.ds(hp * 128, 128)
        for d in (2, 1, 3, 0):
            block = ctxt[:, row_block(peer_at[d])].T.astype(BF16)
            if d:
                slot = hp * nx + d
                cxs[hp, d] = block
                cx_sends[hp, d] = send(
                    cxs.at[hp, d], cx.at[d, :, lanes], s_cx.at[slot], r_cx.at[slot], (c, peer_at[d])
                )
            else:
                cx[0, :, lanes] = block

        for part in (0, 1):
            k0 = part * kc
            keys_at = pl.ds(k0, kc)
            slot = hp * 2 + part

            def near_grads(j, carry):
                grads(1 + 2 * j, 0, PREV + j, hp, k0, 0, seq)
                return carry

            lax.fori_loop(0, 2, near_grads, 0)
            pass_back()
            if part == 0:
                st.wait_recv()
            grads(4, far, PREVX + core, hp, k0, 0, seq)
            pp_s[hp, keys_at, :] = dkv[PREVX, hp, keys_at, :].astype(BF16)
            ppg = send(
                pp_s.at[hp, keys_at, :], pp_r.at[hp, keys_at, :], s_gr.at[slot], r_gr.at[slot], (pair, x)
            )
            sp_s[hp, keys_at, :] = dkv[PAIR, hp, keys_at, :].astype(BF16)
            sent[hp].append(
                send(
                    sp_s.at[hp, keys_at, :], sp_r.at[hp, keys_at, :],
                    s_gr.at[4 + slot], r_gr.at[4 + slot], (pair, x),
                )
            )
            grads(2, 1, PREV, hp, *UPPER[part])
            waiting.append((hp, part, ppg))
            if part == 1:
                dqf_s[hp] = dqt[1, hp].astype(BF16)
                dqf_sends[hp] = send(
                    dqf_s.at[hp], dqf_r.at[hp], s_gr.at[12 + hp], r_gr.at[12 + hp], (ahead, x)
                )
                if hp == 1:
                    give(0)
                grads(0, 0, OWN, hp, *LOWER[1])
                pass_back()
                grads(0, 0, OWN, hp, *LOWER[0])
    give(1)

    def take(group, d):
        if d:
            g_sends[group, d].wait_recv()
        if group == 1:
            return nt(g[1, d], w3[0, :, columns(source[d])])
        cols = pl.ds(pl.multiple_of(source[d] * width + (group // 2) * 128, 128), 128)
        return nt(g[group, d, :, 0:128], w3[1, :, cols]) + nt(g[group, d, :, 128:256], w3[2, :, cols])

    acc = nn(cx[0], wout[columns(x), :])
    for d in ways:
        for hp in (0, 1):
            cx_sends[hp, d].wait_recv()
        acc = acc + nn(cx[d], wout[columns(source[d]), :])
    att_out[...] = acc.astype(BF16)
    gacc[...] = take(0, 0) + take(1, 0)
    for d in ways:
        gacc[...] += take(0, d)
    give(2)
    for d in ways:
        gacc[...] += take(1, d)
    gacc[...] += take(2, 0)
    for d in ways:
        gacc[...] += take(2, d)
    gm[pl.ds(HALO, rows), :] = gacc[...].astype(BF16)
    convolve(gm, exchange_edges(gm, 2), ig_out, True)

    for copy in started:
        copy.wait_send()


def settle_kernel(a_hbm, b_hbm, a_out, b_out, held, sems):
    ins = [pltpu.make_async_copy(src, held.at[i], sems.at[i]) for i, src in enumerate((a_hbm, b_hbm))]
    outs = [pltpu.make_async_copy(held.at[i], dst, sems.at[2 + i]) for i, dst in enumerate((a_out, b_out))]
    for copy in ins:
        copy.start()
    for first, second in zip(ins, outs):
        first.wait()
        second.start()
    for copy in outs:
        copy.wait()


def on_device(tokens, conv_kernel, w_qkv, w_out, lengths, cotangent):
    rows, model = tokens.shape
    vmem = lambda shape, dtype: pltpu.VMEM(shape, dtype)
    dma = lambda count: pltpu.SemaphoreType.DMA((count,))
    scratch = [
        vmem((rows + 2 * HALO, model), BF16),
        vmem((rows + 2 * HALO, model), F32),
        vmem((KS, rows, 128), F32),
        vmem((rows, model), BF16),
        vmem((3, model, model), BF16),
        vmem((model, model), BF16),
        vmem((rows, model), BF16),
        vmem((4, 2, rows, 256), BF16),
        vmem((4, 2, rows, 128), BF16),
        vmem((4, rows, 256), BF16),
        vmem((4, 2, 512, 256), BF16),
        vmem((2, 2, 512, 128), BF16),
        vmem((2, 512, 256), BF16),
        vmem((4, 2, 128, 512), BF16),
        vmem((4, 2, 128, 512), BF16),
        vmem((2, 4, 512, 128), BF16),
        vmem((2, 4, 512, 128), BF16),
        vmem((2, 8, 512), I32),
        vmem((5, 4, 512, 512), F32),
        vmem((2, 2, 128, 512), F32),
        vmem((2, 4, 1, 512), F32),
        vmem((2, 128, 512), BF16),
        vmem((2, 128, 512), BF16),
        vmem((2, 8, 512), F32),
        vmem((2, 8, 512), F32),
        vmem((2, 2, 8, 512), F32),
        vmem((2, 8, 512), F32),
        vmem((128, 512), F32),
        vmem((2, 4, rows, 128), BF16),
        vmem((4, rows, 256), BF16),
        vmem((4, 2, 512, 256), F32),
        vmem((2, 2, 128, 512), F32),
        vmem((2, 512, 256), BF16),
        vmem((2, 512, 256), BF16),
        vmem((2, 512, 256), BF16),
        vmem((2, 512, 256), BF16),
        vmem((2, 512, 256), BF16),
        vmem((2, 512, 256), BF16),
        vmem((2, 128, 512), BF16),
        vmem((2, 128, 512), BF16),
        vmem((3, 4, rows, 256), BF16),
        vmem((3, 4, rows, 256), BF16),
        vmem((rows + 2 * HALO, model), BF16),
        vmem((rows, model), F32),
        vmem(conv_kernel.shape, F32),
        pltpu.SMEM(lengths.shape, I32),
        dma(8),
    ]
    for count in (4, 8, 8, 8, 8, 8, 4, 8, 7, 8, 14, 12):
        scratch += [dma(count), dma(count)]
    whole = pl.BlockSpec(memory_space=pltpu.VMEM)
    anywhere = pl.BlockSpec(memory_space=pl.ANY)
    out = jax.ShapeDtypeStruct((rows, model), BF16)
    attended, input_grad = pl.pallas_call(
        functools.partial(layer_kernel, lax.axis_size("ctx")),
        out_shape=(out, out),
        in_specs=[anywhere] * 6,
        out_specs=(whole, whole),
        scratch_shapes=scratch,
        compiler_params=pltpu.CompilerParams(
            collective_id=0, has_side_effects=True, vmem_limit_bytes=66_000_000
        ),
    )(tokens, cotangent, w_qkv, w_out, conv_kernel, lengths)
    return pl.pallas_call(
        settle_kernel,
        out_shape=(out, out),
        in_specs=[anywhere] * 2,
        out_specs=(anywhere, anywhere),
        scratch_shapes=[vmem((2, rows, model), BF16), dma(4)],
    )(attended, input_grad)


def solution(mesh):
    placed = (P(("ctx", "head"), None), P(), P(), P(), P(), P(("ctx", "head"), None))
    return jax.shard_map(
        on_device,
        mesh=mesh,
        in_specs=placed,
        out_specs=(P(("ctx", "head"), None), P(("ctx", "head"), None)),
        check_vma=False,
    )
```

```python
import functools
import math

import jax
import jax.numpy as jnp
from jax import lax
from jax.experimental import pallas as pl
from jax.experimental.pallas import tpu as pltpu
from jax.sharding import PartitionSpec as P

HD = 64
KS = 7
HALO = 16
OWN, PREV, PREVX, PAIR = 0, 1, 2, 3
MESH = pl.DeviceIdType.MESH
F32, BF16, I32 = jnp.float32, jnp.bfloat16, jnp.int32


def nt(a, b):
    return lax.dot_general(a, b, (((1,), (1,)), ((), ())), preferred_element_type=F32)


def nn(a, b):
    return jnp.dot(a, b, preferred_element_type=F32)


def layer_kernel(
    n_ctx,
    tok_hbm,
    cot_hbm,
    wqkv_hbm,
    wout_hbm,
    convk_hbm,
    lens_hbm,
    att_out,
    ig_out,
    ext,
    ext32,
    cmask,
    cot,
    w3,
    wout,
    mixed,
    kvs,
    qs,
    ds_,
    kv,
    q,
    do,
    kt,
    vt,
    qm,
    dm,
    starts,
    e_ref,
    ot,
    tot,
    of_s,
    of_r,
    tf_s,
    tf_r,
    stat,
    st_s,
    ctxt,
    cxs,
    cx,
    dkv,
    dqt,
    pp_s,
    pp_r,
    sp_s,
    sp_r,
    ps_s,
    ps_r,
    dqf_s,
    dqf_r,
    gs,
    g,
    gm,
    gacc,
    convk,
    lens,
    ld,
    s_h,
    r_h,
    s_kv,
    r_kv,
    s_z,
    r_z,
    s_sp,
    r_sp,
    s_pp,
    r_pp,
    s_q,
    r_q,
    s_d,
    r_d,
    s_qf,
    r_qf,
    s_f,
    r_f,
    s_cx,
    r_cx,
    s_gr,
    r_gr,
    s_g,
    r_g,
):
    c, x = lax.axis_index("ctx"), lax.axis_index("head")
    core = lax.rem(c, 2)
    ahead = lax.rem(c + 2, n_ctx)
    behind = lax.rem(c + n_ctx - 2, n_ctx)
    pair = c + 1 - 2 * core
    rows, width = 128, 256
    seq = 512
    nx = 4
    model = 1024

    up_x = lax.rem(x + 1, nx)
    up_c = lax.rem(c + (x + 1) // nx, n_ctx)
    dn_x = lax.rem(x + nx - 1, nx)
    dn_c = lax.rem(c + n_ctx - (nx - x) // nx, n_ctx)

    loads = [
        pltpu.make_async_copy(tok_hbm, ext.at[pl.ds(HALO, rows), :], ld.at[0]),
        pltpu.make_async_copy(lens_hbm, lens, ld.at[1]),
        pltpu.make_async_copy(convk_hbm, convk, ld.at[2]),
        pltpu.make_async_copy(wqkv_hbm.at[:, pl.ds(model, model)], w3.at[1], ld.at[3]),
        pltpu.make_async_copy(wqkv_hbm.at[:, pl.ds(2 * model, model)], w3.at[2], ld.at[4]),
        pltpu.make_async_copy(wqkv_hbm.at[:, pl.ds(0, model)], w3.at[0], ld.at[5]),
        pltpu.make_async_copy(cot_hbm, cot, ld.at[6]),
        pltpu.make_async_copy(wout_hbm, wout, ld.at[7]),
    ]
    barrier = pltpu.get_barrier_semaphore()
    peers = [(c, lax.rem(x + d, nx)) for d in (1, 2, 3)]
    peers += [(ahead, x), (behind, x), (pair, x), (up_c, up_x), (dn_c, dn_x)]
    for peer in peers:
        pl.semaphore_signal(barrier, inc=1, device_id=peer, device_id_type=MESH)
    for load in loads:
        load.start()
    loads[0].wait()
    pl.semaphore_wait(barrier, len(peers))

    started = []

    def send(src, dst, ss, rs, peer):
        copy = pltpu.make_async_remote_copy(
            src_ref=src, dst_ref=dst, send_sem=ss, recv_sem=rs, device_id=peer, device_id_type=MESH
        )
        copy.start()
        started.append(copy)
        return copy

    def exchange_edges(buf, base):
        up = send(
            buf.at[pl.ds(rows, HALO), :], buf.at[pl.ds(0, HALO), :],
            s_h.at[base], r_h.at[base], (up_c, up_x),
        )
        down = send(
            buf.at[pl.ds(HALO, HALO), :], buf.at[pl.ds(HALO + rows, HALO), :],
            s_h.at[base + 1], r_h.at[base + 1], (dn_c, dn_x),
        )
        return up, down

    edges = exchange_edges(ext, 0)

    loads[1].wait()
    ends = []
    run = jnp.int32(0)
    for i in range(lens.shape[0]):
        run = run + lens[i]
        ends.append(run)
    row_pos = (c * nx + x) * rows + lax.broadcasted_iota(I32, (rows, 128), 0)
    first = jnp.zeros((rows, 128), I32)
    for end in ends:
        first = jnp.where(row_pos >= end, end, first)
    last = jnp.zeros((rows, 128), I32)
    for end in reversed(ends):
        last = jnp.where(row_pos < end, end, last)
    for t in range(KS):
        near = row_pos + (t - KS // 2)
        cmask[t] = jnp.where((near >= first) & (near < last), 1.0, 0.0).astype(F32)

    def columns(p):
        return pl.ds(pl.multiple_of(p * width, width), width)

    def row_block(p):
        return pl.ds(pl.multiple_of(p * rows, rows), rows)

    peer_at = [lax.rem(x + d, nx) for d in range(nx)]
    source = [lax.rem(x + nx - d, nx) for d in range(nx)]
    mine = row_block(x)
    ways = (1, 3, 2)

    def convolve(buf, edges, out, flip):
        def part(at, count):
            def chunk(i, carry):
                lanes = pl.ds(pl.multiple_of(i * 128, 128), 128)
                acc = ext32[pl.ds(HALO + at, count), lanes]
                for t in range(KS):
                    tap = convk[pl.ds(KS - 1 - t if flip else t, 1), lanes]
                    near = ext32[pl.ds(HALO + at - KS // 2 + t, count), lanes]
                    acc = acc + tap * near * cmask[t, pl.ds(at, count), :]
                out[pl.ds(at, count), lanes] = acc.astype(BF16)
                return carry

            lax.fori_loop(0, model // 128, chunk, 0)

        inner = pl.ds(HALO, rows)
        ext32[inner, :] = buf[inner, :].astype(F32)
        part(HALO, rows - 2 * HALO)
        for edge in edges:
            edge.wait_recv()
        for side in (0, HALO + rows):
            ext32[pl.ds(side, HALO), :] = buf[pl.ds(side, HALO), :].astype(F32)
        part(0, HALO)
        part(rows - HALO, HALO)

    loads[2].wait()
    convolve(ext, edges, mixed, False)

    kv_sends, z_sends, sp_sends, pp_sends, q_sends, d_sends, qf_sends = {}, {}, {}, {}, {}, {}, {}

    def give_kv(hp, d):
        slot = hp * nx + d
        kv_sends[hp, d] = send(
            kvs.at[d, hp], kv.at[OWN, hp, mine, :], s_kv.at[slot], r_kv.at[slot], (c, peer_at[d])
        )

    def forward(hp, d):
        at, slot = row_block(source[d]), hp * nx + d
        block = kv.at[OWN, hp, at, :]
        z_sends[hp, d] = send(block, kv.at[PREV, hp, at, :], s_z.at[slot], r_z.at[slot], (ahead, x))
        sp_sends[hp, d] = send(block, kv.at[PAIR, hp, at, :], s_sp.at[slot], r_sp.at[slot], (pair, x))

    def forward_pair(hp, d):
        at, slot = row_block(source[d]), hp * nx + d
        pp_sends[hp, d] = send(
            kv.at[PREV, hp, at, :], kv.at[PREVX, hp, at, :], s_pp.at[slot], r_pp.at[slot], (pair, x)
        )

    def forward_q(hp, d):
        at, slot = row_block(source[d]), hp * nx + d
        qf_sends[hp, d] = send(
            q.at[0, hp, at, :], q.at[1, hp, at, :], s_qf.at[slot], r_qf.at[slot], (behind, x)
        )

    def give_q(hp, d):
        slot = hp * nx + d
        q_sends[hp, d] = send(
            qs.at[d, hp], q.at[0, hp, mine, :], s_q.at[slot], r_q.at[slot], (c, peer_at[d])
        )

    loads[3].wait()
    loads[4].wait()
    for d in (2, 1, 3, 0):
        for part in (0, 1):
            block = nn(mixed[...], w3[1 + part, :, columns(peer_at[d])]).astype(BF16)
            for hp in (0, 1):
                piece = block[:, hp * 128 : hp * 128 + 128]
                if d:
                    kvs[d, hp, :, part * 128 : part * 128 + 128] = piece
                else:
                    kv[OWN, hp, mine, part * 128 : part * 128 + 128] = piece
        if d:
            give_kv(0, d)
    forward(0, 0)
    loads[5].wait()
    for d in (2, 1, 3, 0):
        block = nn(mixed[...], w3[0, :, columns(peer_at[d])]).astype(BF16)
        for hp in (0, 1):
            piece = block[:, hp * 128 : hp * 128 + 128]
            if d:
                qs[d, hp] = piece
            else:
                q[0, hp, mine, :] = piece
        if d:
            give_q(0, d)
    forward_q(0, 0)

    loads[6].wait()
    loads[7].wait()
    for d in (2, 1, 3, 0):
        block = nt(cot[...], wout[columns(peer_at[d]), :]).astype(BF16)
        if d:
            ds_[d] = block
        else:
            do[0, mine, :] = block
    for d in ways:
        kv_sends[0, d].wait_recv()
        forward(0, d)
    ot[...] = jnp.zeros_like(ot)
    tot[...] = jnp.zeros_like(tot)
    dqt[...] = jnp.zeros_like(dqt)
    dkv[...] = jnp.zeros_like(dkv)
    lane = lax.broadcasted_iota(I32, (8, seq), 1)
    for qi, shard in ((0, c), (1, ahead)):
        pos = shard * seq + lane
        first = jnp.zeros((8, seq), I32)
        for end in ends:
            first = jnp.where(pos >= end, end, first)
        starts[qi] = first
    half = lax.broadcasted_iota(I32, (seq, 128), 1) // HD
    for d in ways:
        q_sends[0, d].wait_recv()
        forward_q(0, d)
    for d in (2, 1, 3):
        give_kv(1, d)
    forward(1, 0)
    for d in (2, 1, 3):
        give_q(1, d)
    forward_q(1, 0)
    for d in (2, 1, 3):
        d_sends[d] = send(ds_.at[d], do.at[0, mine, :], s_d.at[d], r_d.at[d], (c, peer_at[d]))

    def split_pair(block, dst, qi, hp):
        block = block.astype(F32)
        for s in (0, 1):
            dst[qi, hp * 2 + s] = jnp.where(half == s, block, 0.0).astype(BF16)

    def turn(slot, hp):
        kt[slot, hp] = kv[slot, hp, :, 0:128].astype(F32).T.astype(BF16)
        vt[slot, hp] = kv[slot, hp, :, 128:256].astype(F32).T.astype(BF16)

    scale = HD ** -0.5
    scale2 = scale * math.log2(math.e)
    kc = 256
    FULL = ((0, 0, seq), (kc, 0, seq))
    LOWER = ((0, 0, seq), (kc, kc, seq - kc))
    UPPER = ((0, 0, kc), (kc, 0, seq))

    def over_parts(parts, tile):
        if parts is FULL:

            def step(part, carry):
                tile(pl.multiple_of(part * kc, kc), 0, seq)
                return carry

            lax.fori_loop(0, seq // kc, step, 0)
        else:
            for part in parts:
                tile(*part)

    def attend(block, qi, slot, distance, parts, hp):
        base = (jnp.where(qi == 0, c, ahead) - distance) * seq

        def tile(k0, q0, queries):
            at = pl.ds(q0, queries)
            keys = kv[slot, hp, pl.ds(k0, kc), 0:128]
            k_iota = lax.broadcasted_iota(I32, (kc, queries), 0)
            ok = base + k0 + k_iota >= starts[qi, 0:1, at]
            if parts is LOWER:
                q_iota = lax.broadcasted_iota(I32, (kc, queries), 1)
                ok = ok & (k0 + k_iota <= q0 + q_iota)
            for s in (0, 1):
                h = hp * 2 + s
                score = nt(keys, qm[qi, h, at, :])
                e = jnp.where(ok, jnp.exp2(score * scale2), 0.0)
                e_ref[block, h, pl.ds(k0, kc), at] = e
                tot[qi, h, :, at] += jnp.sum(e, axis=0, keepdims=True)
                head_rows = pl.ds(s * HD, HD)
                ot[qi, hp, head_rows, at] += nn(vt[slot, hp, head_rows, pl.ds(k0, kc)], e.astype(BF16))

        over_parts(parts, tile)

    def grads(block, qi, slot, hp, k0, q0, queries):
        at = pl.ds(q0, queries)
        keys_at = pl.ds(k0, kc)
        values = kv[slot, hp, keys_at, 128:256]
        for s in (0, 1):
            h = hp * 2 + s
            prob = e_ref[block, h, keys_at, at] * stat[qi, hp, s : s + 1, at]
            d_prob = nt(values, dm[qi, h, at, :])
            d_score = (prob * (d_prob - stat[qi, hp, 4 + s : 5 + s, at])).astype(BF16)
            dkv[slot, hp, keys_at, 128:256] += nn(prob.astype(BF16), dm[qi, h, at, :])
            dkv[slot, hp, keys_at, 0:128] += nn(d_score, qm[qi, h, at, :])
            head_rows = pl.ds(s * HD, HD)
            dqt[qi, hp, head_rows, at] += nn(kt[slot, hp, head_rows, keys_at], d_score)

    far = 1 - core
    def pass_pair(hp):
        for d in (0, 1, 3, 2):
            z_sends[hp, d].wait_recv()
            forward_pair(hp, d)

    def pass_on(d):
        kv_sends[1, d].wait_recv()
        forward(1, d)
        q_sends[1, d].wait_recv()
        forward_q(1, d)

    of_sends = []
    for hp in (0, 1):
        split_pair(q[0, hp], qm, 0, hp)
        turn(OWN, hp)
        attend(0, 0, OWN, 0, LOWER, hp)
        if hp == 1:
            for d in ways:
                d_sends[d].wait_recv()
            df = send(do.at[0], do.at[1], s_f.at[0], r_f.at[0], (behind, x))
        pass_pair(hp)
        for d in range(nx):
            qf_sends[hp, d].wait_recv()
        split_pair(q[1, hp], qm, 1, hp)
        turn(PREV, hp)
        attend(2, 1, PREV, 4, UPPER, hp)
        if hp == 0:
            pass_on(1)
            pass_on(3)
        attend(1, 0, PREV, 2, FULL, hp)
        if hp == 0:
            pass_on(2)
        for d in range(nx):
            pp_sends[hp, d].wait_recv()
            sp_sends[hp, d].wait_recv()
        turn(PREVX, hp)
        turn(PAIR, hp)

        def crossed(j, carry):
            distance = jnp.where(j == 0, 3 - 2 * core, 1 + 2 * core)
            attend(4 - j, (1 - j) * far, PREVX + (1 - j) * core, distance, FULL, hp)
            return carry

        lax.fori_loop(0, 2, crossed, 0)
        of_s[hp] = ot[1, hp].astype(BF16)
        for s in (0, 1):
            for row in range(4):
                tf_s[hp, row * 2 + s : row * 2 + s + 1, :] = tot[1, hp * 2 + s]
        of_sends.append(
            (
                send(tf_s.at[hp], tf_r.at[hp], s_f.at[1 + hp], r_f.at[1 + hp], (ahead, x)),
                send(of_s.at[hp], of_r.at[hp], s_f.at[3 + hp], r_f.at[3 + hp], (ahead, x)),
            )
        )
    df.wait_recv()
    for qi in (0, 1):
        for hp in (0, 1):
            split_pair(do[qi, :, hp * 128 : hp * 128 + 128], dm, qi, hp)

    g_sends = {}
    sent = [[], []]
    dqf_sends = [None, None]
    waiting = []

    def pass_back():
        while waiting:
            hp, part, ppg = waiting.pop()
            keys_at = pl.ds(part * kc, kc)
            slot = 8 + hp * 2 + part
            ppg.wait_recv()
            ps_s[hp, keys_at, :] = (dkv[PREV, hp, keys_at, :] + pp_r[hp, keys_at, :].astype(F32)).astype(BF16)
            sent[hp].append(
                send(
                    ps_s.at[hp, keys_at, :], ps_r.at[hp, keys_at, :], s_gr.at[slot], r_gr.at[slot], (behind, x)
                )
            )

    def give(group):
        if group == 1:
            for hp in (0, 1):
                dqf_sends[hp].wait_recv()
                dqt[0, hp] = (dqt[0, hp] + dqf_r[hp].astype(F32)) * scale
        else:
            hp = group // 2
            for copy in sent[hp]:
                copy.wait_recv()
        for d in (2, 1, 3, 0):
            at = row_block(peer_at[d])
            out = gs.at[group, d] if d else g.at[group, 0]
            if group == 1:
                for hp in (0, 1):
                    out[:, hp * 128 : hp * 128 + 128] = dqt[0, hp, :, at].T.astype(BF16)
            else:
                hp = group // 2
                total = dkv[OWN, hp, at, :] + ps_r[hp, at, :].astype(F32) + sp_r[hp, at, :].astype(F32)
                out[:, 0:128] = (total[:, 0:128] * scale).astype(BF16)
                out[:, 128:256] = total[:, 128:256].astype(BF16)
            if d:
                slot = group * nx + d
                g_sends[group, d] = send(
                    gs.at[group, d], g.at[group, d], s_g.at[slot], r_g.at[slot], (c, peer_at[d])
                )

    cx_sends = {}
    st_sends = [None, None]

    def context_of(hp):
        for copy in of_sends[hp]:
            copy.wait_recv()
        d_turned = do[0, :, hp * 128 : hp * 128 + 128].astype(F32).T
        for s in (0, 1):
            head_rows = slice(s * HD, (s + 1) * HD)
            total = tot[0, hp * 2 + s] + tf_r[hp, s : s + 1, :]
            whole = ot[0, hp, head_rows, :] + of_r[hp, head_rows, :].astype(F32)
            context = (whole / total).astype(BF16).astype(F32)
            ctxt[head_rows, :] = context
            st_s[hp, s : s + 1, :] = 1.0 / total
            st_s[hp, 4 + s : 5 + s, :] = jnp.sum(d_turned[head_rows, :] * context, axis=0, keepdims=True)
        stat[0, hp] = st_s[hp]
        st_sends[hp] = send(st_s.at[hp], stat.at[1, hp], s_f.at[5 + hp], r_f.at[5 + hp], (behind, x))
        lanes = pl.ds(hp * 128, 128)
        for d in (2, 1, 3, 0):
            block = ctxt[:, row_block(peer_at[d])].T.astype(BF16)
            if d:
                slot = hp * nx + d
                cxs[hp, d] = block
                cx_sends[hp, d] = send(
                    cxs.at[hp, d], cx.at[d, :, lanes], s_cx.at[slot], r_cx.at[slot], (c, peer_at[d])
                )
            else:
                cx[0, :, lanes] = block

    context_of(0)
    for hp in (0, 1):
        if hp == 0:
            for lower in LOWER:
                grads(0, 0, OWN, 0, *lower)
        for part in (0, 1):
            k0 = part * kc
            keys_at = pl.ds(k0, kc)
            slot = hp * 2 + part

            def near_grads(j, carry):
                grads(1 + 2 * j, 0, PREV + j, hp, k0, 0, seq)
                return carry

            lax.fori_loop(0, 2, near_grads, 0)
            pass_back()
            if part == 0:
                st_sends[hp].wait_recv()
            grads(4, far, PREVX + core, hp, k0, 0, seq)
            pp_s[hp, keys_at, :] = dkv[PREVX, hp, keys_at, :].astype(BF16)
            ppg = send(
                pp_s.at[hp, keys_at, :], pp_r.at[hp, keys_at, :], s_gr.at[slot], r_gr.at[slot], (pair, x)
            )
            sp_s[hp, keys_at, :] = dkv[PAIR, hp, keys_at, :].astype(BF16)
            sent[hp].append(
                send(
                    sp_s.at[hp, keys_at, :], sp_r.at[hp, keys_at, :],
                    s_gr.at[4 + slot], r_gr.at[4 + slot], (pair, x),
                )
            )
            grads(2, 1, PREV, hp, *UPPER[part])
            waiting.append((hp, part, ppg))
            if part == 1:
                dqf_s[hp] = dqt[1, hp].astype(BF16)
                dqf_sends[hp] = send(
                    dqf_s.at[hp], dqf_r.at[hp], s_gr.at[12 + hp], r_gr.at[12 + hp], (ahead, x)
                )
                if hp == 1:
                    grads(0, 0, OWN, 1, *LOWER[1])
                    pass_back()
                    give(0)
                    grads(0, 0, OWN, 1, *LOWER[0])
            elif hp == 0:
                context_of(1)
    give(1)

    def take(group, d):
        if d:
            g_sends[group, d].wait_recv()
        if group == 1:
            return nt(g[1, d], w3[0, :, columns(source[d])])
        cols = pl.ds(pl.multiple_of(source[d] * width + (group // 2) * 128, 128), 128)
        return nt(g[group, d, :, 0:128], w3[1, :, cols]) + nt(g[group, d, :, 128:256], w3[2, :, cols])

    acc = nn(cx[0], wout[columns(x), :])
    for d in ways:
        for hp in (0, 1):
            cx_sends[hp, d].wait_recv()
        acc = acc + nn(cx[d], wout[columns(source[d]), :])
    att_out[...] = acc.astype(BF16)
    gacc[...] = take(0, 0) + take(1, 0)
    for d in ways:
        gacc[...] += take(0, d)
    give(2)
    for d in ways:
        gacc[...] += take(1, d)
    gacc[...] += take(2, 0)
    for d in ways:
        gacc[...] += take(2, d)
    gm[pl.ds(HALO, rows), :] = gacc[...].astype(BF16)
    convolve(gm, exchange_edges(gm, 2), ig_out, True)

    for copy in started:
        copy.wait_send()


def settle_kernel(a_hbm, b_hbm, a_out, b_out, held, sems):
    ins = [pltpu.make_async_copy(src, held.at[i], sems.at[i]) for i, src in enumerate((a_hbm, b_hbm))]
    outs = [pltpu.make_async_copy(held.at[i], dst, sems.at[2 + i]) for i, dst in enumerate((a_out, b_out))]
    for copy in ins:
        copy.start()
    for first, second in zip(ins, outs):
        first.wait()
        second.start()
    for copy in outs:
        copy.wait()


def on_device(tokens, conv_kernel, w_qkv, w_out, lengths, cotangent):
    rows, model = tokens.shape
    vmem = lambda shape, dtype: pltpu.VMEM(shape, dtype)
    dma = lambda count: pltpu.SemaphoreType.DMA((count,))
    scratch = [
        vmem((rows + 2 * HALO, model), BF16),
        vmem((rows + 2 * HALO, model), F32),
        vmem((KS, rows, 128), F32),
        vmem((rows, model), BF16),
        vmem((3, model, model), BF16),
        vmem((model, model), BF16),
        vmem((rows, model), BF16),
        vmem((4, 2, rows, 256), BF16),
        vmem((4, 2, rows, 128), BF16),
        vmem((4, rows, 256), BF16),
        vmem((4, 2, 512, 256), BF16),
        vmem((2, 2, 512, 128), BF16),
        vmem((2, 512, 256), BF16),
        vmem((4, 2, 128, 512), BF16),
        vmem((4, 2, 128, 512), BF16),
        vmem((2, 4, 512, 128), BF16),
        vmem((2, 4, 512, 128), BF16),
        vmem((2, 8, 512), I32),
        vmem((5, 4, 512, 512), F32),
        vmem((2, 2, 128, 512), F32),
        vmem((2, 4, 1, 512), F32),
        vmem((2, 128, 512), BF16),
        vmem((2, 128, 512), BF16),
        vmem((2, 8, 512), F32),
        vmem((2, 8, 512), F32),
        vmem((2, 2, 8, 512), F32),
        vmem((2, 8, 512), F32),
        vmem((128, 512), F32),
        vmem((2, 4, rows, 128), BF16),
        vmem((4, rows, 256), BF16),
        vmem((4, 2, 512, 256), F32),
        vmem((2, 2, 128, 512), F32),
        vmem((2, 512, 256), BF16),
        vmem((2, 512, 256), BF16),
        vmem((2, 512, 256), BF16),
        vmem((2, 512, 256), BF16),
        vmem((2, 512, 256), BF16),
        vmem((2, 512, 256), BF16),
        vmem((2, 128, 512), BF16),
        vmem((2, 128, 512), BF16),
        vmem((3, 4, rows, 256), BF16),
        vmem((3, 4, rows, 256), BF16),
        vmem((rows + 2 * HALO, model), BF16),
        vmem((rows, model), F32),
        vmem(conv_kernel.shape, F32),
        pltpu.SMEM(lengths.shape, I32),
        dma(8),
    ]
    for count in (4, 8, 8, 8, 8, 8, 4, 8, 7, 8, 14, 12):
        scratch += [dma(count), dma(count)]
    whole = pl.BlockSpec(memory_space=pltpu.VMEM)
    anywhere = pl.BlockSpec(memory_space=pl.ANY)
    out = jax.ShapeDtypeStruct((rows, model), BF16)
    attended, input_grad = pl.pallas_call(
        functools.partial(layer_kernel, lax.axis_size("ctx")),
        out_shape=(out, out),
        in_specs=[anywhere] * 6,
        out_specs=(whole, whole),
        scratch_shapes=scratch,
        compiler_params=pltpu.CompilerParams(
            collective_id=0, has_side_effects=True, vmem_limit_bytes=66_000_000
        ),
    )(tokens, cotangent, w_qkv, w_out, conv_kernel, lengths)
    return pl.pallas_call(
        settle_kernel,
        out_shape=(out, out),
        in_specs=[anywhere] * 2,
        out_specs=(anywhere, anywhere),
        scratch_shapes=[vmem((2, rows, model), BF16), dma(4)],
    )(attended, input_grad)


def solution(mesh):
    placed = (P(("ctx", "head"), None), P(), P(), P(), P(), P(("ctx", "head"), None))
    return jax.shard_map(
        on_device,
        mesh=mesh,
        in_specs=placed,
        out_specs=(P(("ctx", "head"), None), P(("ctx", "head"), None)),
        check_vma=False,
    )
```

```python
import functools
import math

import jax
import jax.numpy as jnp
from jax import lax
from jax.experimental import pallas as pl
from jax.experimental.pallas import tpu as pltpu
from jax.sharding import PartitionSpec as P

HD = 64
KS = 7
HALO = 16
OWN, PREV, PREVX, PAIR = 0, 1, 2, 3
MESH = pl.DeviceIdType.MESH
F32, BF16, I32 = jnp.float32, jnp.bfloat16, jnp.int32


def nt(a, b):
    return lax.dot_general(a, b, (((1,), (1,)), ((), ())), preferred_element_type=F32)


def nn(a, b):
    return jnp.dot(a, b, preferred_element_type=F32)


def layer_kernel(
    n_ctx,
    tok_hbm,
    cot_hbm,
    wqkv_hbm,
    wout_hbm,
    convk_hbm,
    lens_hbm,
    att_out,
    ig_out,
    ext,
    ext32,
    cmask,
    cot,
    w3,
    wout,
    mixed,
    kvs,
    qs,
    ds_,
    kv,
    q,
    do,
    kt,
    vt,
    qm,
    dm,
    starts,
    e_ref,
    ot,
    tot,
    of_s,
    of_r,
    tf_s,
    tf_r,
    stat,
    st_s,
    ctxt,
    cxs,
    cx,
    dkv,
    dqt,
    pp_s,
    pp_r,
    sp_s,
    sp_r,
    ps_s,
    ps_r,
    dqf_s,
    dqf_r,
    gs,
    g,
    gm,
    gacc,
    convk,
    lens,
    ld,
    s_h,
    r_h,
    s_kv,
    r_kv,
    s_z,
    r_z,
    s_sp,
    r_sp,
    s_pp,
    r_pp,
    s_q,
    r_q,
    s_d,
    r_d,
    s_qf,
    r_qf,
    s_f,
    r_f,
    s_cx,
    r_cx,
    s_gr,
    r_gr,
    s_g,
    r_g,
):
    c, x = lax.axis_index("ctx"), lax.axis_index("head")
    core = lax.rem(c, 2)
    ahead = lax.rem(c + 2, n_ctx)
    behind = lax.rem(c + n_ctx - 2, n_ctx)
    pair = c + 1 - 2 * core
    rows, width = 128, 256
    seq = 512
    nx = 4
    model = 1024

    up_x = lax.rem(x + 1, nx)
    up_c = lax.rem(c + (x + 1) // nx, n_ctx)
    dn_x = lax.rem(x + nx - 1, nx)
    dn_c = lax.rem(c + n_ctx - (nx - x) // nx, n_ctx)

    loads = [
        pltpu.make_async_copy(tok_hbm, ext.at[pl.ds(HALO, rows), :], ld.at[0]),
        pltpu.make_async_copy(lens_hbm, lens, ld.at[1]),
        pltpu.make_async_copy(convk_hbm, convk, ld.at[2]),
        pltpu.make_async_copy(wqkv_hbm.at[:, pl.ds(model, model)], w3.at[1], ld.at[3]),
        pltpu.make_async_copy(wqkv_hbm.at[:, pl.ds(2 * model, model)], w3.at[2], ld.at[4]),
        pltpu.make_async_copy(wqkv_hbm.at[:, pl.ds(0, model)], w3.at[0], ld.at[5]),
        pltpu.make_async_copy(cot_hbm, cot, ld.at[6]),
        pltpu.make_async_copy(wout_hbm, wout, ld.at[7]),
    ]
    barrier = pltpu.get_barrier_semaphore()
    peers = [(c, lax.rem(x + d, nx)) for d in (1, 2, 3)]
    peers += [(ahead, x), (behind, x), (pair, x), (up_c, up_x), (dn_c, dn_x)]
    for peer in peers:
        pl.semaphore_signal(barrier, inc=1, device_id=peer, device_id_type=MESH)
    for load in loads:
        load.start()
    loads[0].wait()
    pl.semaphore_wait(barrier, len(peers))

    started = []

    def send(src, dst, ss, rs, peer):
        copy = pltpu.make_async_remote_copy(
            src_ref=src, dst_ref=dst, send_sem=ss, recv_sem=rs, device_id=peer, device_id_type=MESH
        )
        copy.start()
        started.append(copy)
        return copy

    def exchange_edges(buf, base):
        up = send(
            buf.at[pl.ds(rows, HALO), :], buf.at[pl.ds(0, HALO), :],
            s_h.at[base], r_h.at[base], (up_c, up_x),
        )
        down = send(
            buf.at[pl.ds(HALO, HALO), :], buf.at[pl.ds(HALO + rows, HALO), :],
            s_h.at[base + 1], r_h.at[base + 1], (dn_c, dn_x),
        )
        return up, down

    edges = exchange_edges(ext, 0)

    loads[1].wait()
    ends = []
    run = jnp.int32(0)
    for i in range(lens.shape[0]):
        run = run + lens[i]
        ends.append(run)
    row_pos = (c * nx + x) * rows + lax.broadcasted_iota(I32, (rows, 128), 0)
    first = jnp.zeros((rows, 128), I32)
    for end in ends:
        first = jnp.where(row_pos >= end, end, first)
    last = jnp.zeros((rows, 128), I32)
    for end in reversed(ends):
        last = jnp.where(row_pos < end, end, last)
    for t in range(KS):
        near = row_pos + (t - KS // 2)
        cmask[t] = jnp.where((near >= first) & (near < last), 1.0, 0.0).astype(F32)

    def columns(p):
        return pl.ds(pl.multiple_of(p * width, width), width)

    def row_block(p):
        return pl.ds(pl.multiple_of(p * rows, rows), rows)

    peer_at = [lax.rem(x + d, nx) for d in range(nx)]
    source = [lax.rem(x + nx - d, nx) for d in range(nx)]
    mine = row_block(x)
    ways = (1, 3, 2)

    def convolve(buf, edges, out, flip):
        def part(at, count):
            def chunk(i, carry):
                lanes = pl.ds(pl.multiple_of(i * 128, 128), 128)
                acc = ext32[pl.ds(HALO + at, count), lanes]
                for t in range(KS):
                    tap = convk[pl.ds(KS - 1 - t if flip else t, 1), lanes]
                    near = ext32[pl.ds(HALO + at - KS // 2 + t, count), lanes]
                    acc = acc + tap * near * cmask[t, pl.ds(at, count), :]
                out[pl.ds(at, count), lanes] = acc.astype(BF16)
                return carry

            lax.fori_loop(0, model // 128, chunk, 0)

        inner = pl.ds(HALO, rows)
        ext32[inner, :] = buf[inner, :].astype(F32)
        part(HALO, rows - 2 * HALO)
        for edge in edges:
            edge.wait_recv()
        for side in (0, HALO + rows):
            ext32[pl.ds(side, HALO), :] = buf[pl.ds(side, HALO), :].astype(F32)
        part(0, HALO)
        part(rows - HALO, HALO)

    loads[2].wait()
    convolve(ext, edges, mixed, False)

    kv_sends, z_sends, sp_sends, pp_sends, q_sends, d_sends, qf_sends = {}, {}, {}, {}, {}, {}, {}

    def give_kv(hp, d):
        slot = hp * nx + d
        kv_sends[hp, d] = send(
            kvs.at[d, hp], kv.at[OWN, hp, mine, :], s_kv.at[slot], r_kv.at[slot], (c, peer_at[d])
        )

    def forward(hp, d):
        at, slot = row_block(source[d]), hp * nx + d
        block = kv.at[OWN, hp, at, :]
        z_sends[hp, d] = send(block, kv.at[PREV, hp, at, :], s_z.at[slot], r_z.at[slot], (ahead, x))
        sp_sends[hp, d] = send(block, kv.at[PAIR, hp, at, :], s_sp.at[slot], r_sp.at[slot], (pair, x))

    def forward_pair(hp, d):
        at, slot = row_block(source[d]), hp * nx + d
        pp_sends[hp, d] = send(
            kv.at[PREV, hp, at, :], kv.at[PREVX, hp, at, :], s_pp.at[slot], r_pp.at[slot], (pair, x)
        )

    def forward_q(hp, d):
        at, slot = row_block(source[d]), hp * nx + d
        qf_sends[hp, d] = send(
            q.at[0, hp, at, :], q.at[1, hp, at, :], s_qf.at[slot], r_qf.at[slot], (behind, x)
        )

    def give_q(hp, d):
        slot = hp * nx + d
        q_sends[hp, d] = send(
            qs.at[d, hp], q.at[0, hp, mine, :], s_q.at[slot], r_q.at[slot], (c, peer_at[d])
        )

    loads[3].wait()
    loads[4].wait()
    for d in (2, 1, 3, 0):
        for part in (0, 1):
            block = nn(mixed[...], w3[1 + part, :, columns(peer_at[d])]).astype(BF16)
            for hp in (0, 1):
                piece = block[:, hp * 128 : hp * 128 + 128]
                if d:
                    kvs[d, hp, :, part * 128 : part * 128 + 128] = piece
                else:
                    kv[OWN, hp, mine, part * 128 : part * 128 + 128] = piece
        if d:
            give_kv(0, d)
    forward(0, 0)
    loads[5].wait()
    for d in (2, 1, 3, 0):
        block = nn(mixed[...], w3[0, :, columns(peer_at[d])]).astype(BF16)
        for hp in (0, 1):
            piece = block[:, hp * 128 : hp * 128 + 128]
            if d:
                qs[d, hp] = piece
            else:
                q[0, hp, mine, :] = piece
        if d:
            give_q(0, d)
    forward_q(0, 0)

    loads[6].wait()
    loads[7].wait()
    for d in (2, 1, 3, 0):
        block = nt(cot[...], wout[columns(peer_at[d]), :]).astype(BF16)
        if d:
            ds_[d] = block
        else:
            do[0, mine, :] = block
    for d in ways:
        kv_sends[0, d].wait_recv()
        forward(0, d)
    ot[...] = jnp.zeros_like(ot)
    tot[...] = jnp.zeros_like(tot)
    dqt[...] = jnp.zeros_like(dqt)
    dkv[...] = jnp.zeros_like(dkv)
    lane = lax.broadcasted_iota(I32, (8, seq), 1)
    for qi, shard in ((0, c), (1, ahead)):
        pos = shard * seq + lane
        first = jnp.zeros((8, seq), I32)
        for end in ends:
            first = jnp.where(pos >= end, end, first)
        starts[qi] = first
    half = lax.broadcasted_iota(I32, (seq, 128), 1) // HD
    for d in ways:
        q_sends[0, d].wait_recv()
        forward_q(0, d)
    for d in (2, 1, 3):
        give_kv(1, d)
    forward(1, 0)
    for d in (2, 1, 3):
        give_q(1, d)
    forward_q(1, 0)
    for d in (2, 1, 3):
        d_sends[d] = send(ds_.at[d], do.at[0, mine, :], s_d.at[d], r_d.at[d], (c, peer_at[d]))

    def split_pair(block, dst, qi, hp):
        block = block.astype(F32)
        for s in (0, 1):
            dst[qi, hp * 2 + s] = jnp.where(half == s, block, 0.0).astype(BF16)

    def turn(slot, hp):
        kt[slot, hp] = kv[slot, hp, :, 0:128].astype(F32).T.astype(BF16)
        vt[slot, hp] = kv[slot, hp, :, 128:256].astype(F32).T.astype(BF16)

    scale = HD ** -0.5
    scale2 = scale * math.log2(math.e)
    kc = 256
    FULL = ((0, 0, seq), (kc, 0, seq))
    LOWER = ((0, 0, seq), (kc, kc, seq - kc))
    UPPER = ((0, 0, kc), (kc, 0, seq))

    def over_parts(parts, tile):
        if parts is FULL:

            def step(part, carry):
                tile(pl.multiple_of(part * kc, kc), 0, seq)
                return carry

            lax.fori_loop(0, seq // kc, step, 0)
        else:
            for part in parts:
                tile(*part)

    def attend(block, qi, slot, distance, parts, hp):
        base = (jnp.where(qi == 0, c, ahead) - distance) * seq

        def tile(k0, q0, queries):
            at = pl.ds(q0, queries)
            keys = kv[slot, hp, pl.ds(k0, kc), 0:128]
            k_iota = lax.broadcasted_iota(I32, (kc, queries), 0)
            ok = base + k0 + k_iota >= starts[qi, 0:1, at]
            if parts is LOWER:
                q_iota = lax.broadcasted_iota(I32, (kc, queries), 1)
                ok = ok & (k0 + k_iota <= q0 + q_iota)
            for s in (0, 1):
                h = hp * 2 + s
                score = nt(keys, qm[qi, h, at, :])
                e = jnp.where(ok, jnp.exp2(score * scale2), 0.0)
                e_ref[block, h, pl.ds(k0, kc), at] = e
                tot[qi, h, :, at] += jnp.sum(e, axis=0, keepdims=True)
                head_rows = pl.ds(s * HD, HD)
                ot[qi, hp, head_rows, at] += nn(vt[slot, hp, head_rows, pl.ds(k0, kc)], e.astype(BF16))

        over_parts(parts, tile)

    def grads(block, qi, slot, hp, k0, q0, queries):
        at = pl.ds(q0, queries)
        keys_at = pl.ds(k0, kc)
        values = kv[slot, hp, keys_at, 128:256]
        for s in (0, 1):
            h = hp * 2 + s
            prob = e_ref[block, h, keys_at, at] * stat[qi, hp, s : s + 1, at]
            d_prob = nt(values, dm[qi, h, at, :])
            d_score = (prob * (d_prob - stat[qi, hp, 4 + s : 5 + s, at])).astype(BF16)
            dkv[slot, hp, keys_at, 128:256] += nn(prob.astype(BF16), dm[qi, h, at, :])
            dkv[slot, hp, keys_at, 0:128] += nn(d_score, qm[qi, h, at, :])
            head_rows = pl.ds(s * HD, HD)
            dqt[qi, hp, head_rows, at] += nn(kt[slot, hp, head_rows, keys_at], d_score)

    far = 1 - core
    def pass_pair(hp):
        for d in (0, 1, 3, 2):
            z_sends[hp, d].wait_recv()
            forward_pair(hp, d)

    def pass_on(d):
        kv_sends[1, d].wait_recv()
        forward(1, d)
        q_sends[1, d].wait_recv()
        forward_q(1, d)

    of_sends = []
    for hp in (0, 1):
        split_pair(q[0, hp], qm, 0, hp)
        turn(OWN, hp)
        attend(0, 0, OWN, 0, LOWER, hp)
        if hp == 1:
            for d in ways:
                d_sends[d].wait_recv()
            df = send(do.at[0], do.at[1], s_f.at[0], r_f.at[0], (behind, x))
        pass_pair(hp)
        for d in range(nx):
            qf_sends[hp, d].wait_recv()
        split_pair(q[1, hp], qm, 1, hp)
        turn(PREV, hp)
        attend(2, 1, PREV, 4, UPPER, hp)
        if hp == 0:
            pass_on(1)
            pass_on(3)
        attend(1, 0, PREV, 2, FULL, hp)
        if hp == 0:
            pass_on(2)
        for d in range(nx):
            pp_sends[hp, d].wait_recv()
            sp_sends[hp, d].wait_recv()
        turn(PREVX, hp)
        turn(PAIR, hp)

        def crossed(j, carry):
            distance = jnp.where(j == 0, 3 - 2 * core, 1 + 2 * core)
            attend(4 - j, (1 - j) * far, PREVX + (1 - j) * core, distance, FULL, hp)
            return carry

        lax.fori_loop(0, 2, crossed, 0)
        of_s[hp] = ot[1, hp].astype(BF16)
        for s in (0, 1):
            for row in range(4):
                tf_s[hp, row * 2 + s : row * 2 + s + 1, :] = tot[1, hp * 2 + s]
        of_sends.append(
            (
                send(tf_s.at[hp], tf_r.at[hp], s_f.at[1 + hp], r_f.at[1 + hp], (ahead, x)),
                send(of_s.at[hp], of_r.at[hp], s_f.at[3 + hp], r_f.at[3 + hp], (ahead, x)),
            )
        )
    df.wait_recv()
    for qi in (0, 1):
        for hp in (0, 1):
            split_pair(do[qi, :, hp * 128 : hp * 128 + 128], dm, qi, hp)

    g_sends = {}
    sent = [[], []]
    dqf_sends = [None, None]
    waiting = []

    def pass_back():
        while waiting:
            hp, part, ppg = waiting.pop()
            keys_at = pl.ds(part * kc, kc)
            slot = 8 + hp * 2 + part
            ppg.wait_recv()
            ps_s[hp, keys_at, :] = (dkv[PREV, hp, keys_at, :] + pp_r[hp, keys_at, :].astype(F32)).astype(BF16)
            sent[hp].append(
                send(
                    ps_s.at[hp, keys_at, :], ps_r.at[hp, keys_at, :], s_gr.at[slot], r_gr.at[slot], (behind, x)
                )
            )

    def give(group):
        if group == 1:
            for hp in (0, 1):
                dqf_sends[hp].wait_recv()
                dqt[0, hp] = (dqt[0, hp] + dqf_r[hp].astype(F32)) * scale
        else:
            hp = group // 2
            for copy in sent[hp]:
                copy.wait_recv()
        for d in (2, 1, 3, 0):
            at = row_block(peer_at[d])
            out = gs.at[group, d] if d else g.at[group, 0]
            if group == 1:
                for hp in (0, 1):
                    out[:, hp * 128 : hp * 128 + 128] = dqt[0, hp, :, at].T.astype(BF16)
            else:
                hp = group // 2
                total = dkv[OWN, hp, at, :] + ps_r[hp, at, :].astype(F32) + sp_r[hp, at, :].astype(F32)
                out[:, 0:128] = (total[:, 0:128] * scale).astype(BF16)
                out[:, 128:256] = total[:, 128:256].astype(BF16)
            if d:
                slot = group * nx + d
                g_sends[group, d] = send(
                    gs.at[group, d], g.at[group, d], s_g.at[slot], r_g.at[slot], (c, peer_at[d])
                )

    cx_sends = {}
    st_sends = [None, None]

    def context_of(hp):
        for copy in of_sends[hp]:
            copy.wait_recv()
        d_turned = do[0, :, hp * 128 : hp * 128 + 128].astype(F32).T
        for s in (0, 1):
            head_rows = slice(s * HD, (s + 1) * HD)
            total = tot[0, hp * 2 + s] + tf_r[hp, s : s + 1, :]
            whole = ot[0, hp, head_rows, :] + of_r[hp, head_rows, :].astype(F32)
            context = (whole / total).astype(BF16).astype(F32)
            ctxt[head_rows, :] = context
            st_s[hp, s : s + 1, :] = 1.0 / total
            st_s[hp, 4 + s : 5 + s, :] = jnp.sum(d_turned[head_rows, :] * context, axis=0, keepdims=True)
        stat[0, hp] = st_s[hp]
        st_sends[hp] = send(st_s.at[hp], stat.at[1, hp], s_f.at[5 + hp], r_f.at[5 + hp], (behind, x))
        lanes = pl.ds(hp * 128, 128)
        for d in (2, 1, 3, 0):
            block = ctxt[:, row_block(peer_at[d])].T.astype(BF16)
            if d:
                slot = hp * nx + d
                cxs[hp, d] = block
                cx_sends[hp, d] = send(
                    cxs.at[hp, d], cx.at[d, :, lanes], s_cx.at[slot], r_cx.at[slot], (c, peer_at[d])
                )
            else:
                cx[0, :, lanes] = block

    context_of(0)
    for hp in (0, 1):
        if hp == 0:
            for lower in LOWER:
                grads(0, 0, OWN, 0, *lower)
        for part in (0, 1):
            k0 = part * kc
            keys_at = pl.ds(k0, kc)
            slot = hp * 2 + part

            def near_grads(j, carry):
                grads(1 + 2 * j, 0, PREV + j, hp, k0, 0, seq)
                return carry

            lax.fori_loop(0, 2, near_grads, 0)
            pass_back()
            if part == 0:
                st_sends[hp].wait_recv()
            grads(4, far, PREVX + core, hp, k0, 0, seq)
            pp_s[hp, keys_at, :] = dkv[PREVX, hp, keys_at, :].astype(BF16)
            ppg = send(
                pp_s.at[hp, keys_at, :], pp_r.at[hp, keys_at, :], s_gr.at[slot], r_gr.at[slot], (pair, x)
            )
            sp_s[hp, keys_at, :] = dkv[PAIR, hp, keys_at, :].astype(BF16)
            sent[hp].append(
                send(
                    sp_s.at[hp, keys_at, :], sp_r.at[hp, keys_at, :],
                    s_gr.at[4 + slot], r_gr.at[4 + slot], (pair, x),
                )
            )
            grads(2, 1, PREV, hp, *UPPER[part])
            waiting.append((hp, part, ppg))
            if part == 1:
                dqf_s[hp] = dqt[1, hp].astype(BF16)
                dqf_sends[hp] = send(
                    dqf_s.at[hp], dqf_r.at[hp], s_gr.at[12 + hp], r_gr.at[12 + hp], (ahead, x)
                )
                if hp == 1:
                    grads(0, 0, OWN, 1, *LOWER[1])
                    pass_back()
                    give(0)
                    grads(0, 0, OWN, 1, *LOWER[0])
            elif hp == 0:
                context_of(1)
    def take(group, d):
        if d:
            g_sends[group, d].wait_recv()
        if group == 1:
            return nt(g[1, d], w3[0, :, columns(source[d])])
        cols = pl.ds(pl.multiple_of(source[d] * width + (group // 2) * 128, 128), 128)
        return nt(g[group, d, :, 0:128], w3[1, :, cols]) + nt(g[group, d, :, 128:256], w3[2, :, cols])

    acc = nn(cx[0], wout[columns(x), :])
    for d in ways:
        for hp in (0, 1):
            cx_sends[hp, d].wait_recv()
        acc = acc + nn(cx[d], wout[columns(source[d]), :])
    att_out[...] = acc.astype(BF16)
    give(1)
    gacc[...] = take(0, 0) + take(1, 0)
    for d in ways:
        gacc[...] += take(0, d)
    give(2)
    for d in ways:
        gacc[...] += take(1, d)
    gacc[...] += take(2, 0)
    for d in ways:
        gacc[...] += take(2, d)
    gm[pl.ds(HALO, rows), :] = gacc[...].astype(BF16)
    convolve(gm, exchange_edges(gm, 2), ig_out, True)

    for copy in started:
        copy.wait_send()


def settle_kernel(a_hbm, b_hbm, a_out, b_out, held, sems):
    ins = [pltpu.make_async_copy(src, held.at[i], sems.at[i]) for i, src in enumerate((a_hbm, b_hbm))]
    outs = [pltpu.make_async_copy(held.at[i], dst, sems.at[2 + i]) for i, dst in enumerate((a_out, b_out))]
    for copy in ins:
        copy.start()
    for first, second in zip(ins, outs):
        first.wait()
        second.start()
    for copy in outs:
        copy.wait()


def on_device(tokens, conv_kernel, w_qkv, w_out, lengths, cotangent):
    rows, model = tokens.shape
    vmem = lambda shape, dtype: pltpu.VMEM(shape, dtype)
    dma = lambda count: pltpu.SemaphoreType.DMA((count,))
    scratch = [
        vmem((rows + 2 * HALO, model), BF16),
        vmem((rows + 2 * HALO, model), F32),
        vmem((KS, rows, 128), F32),
        vmem((rows, model), BF16),
        vmem((3, model, model), BF16),
        vmem((model, model), BF16),
        vmem((rows, model), BF16),
        vmem((4, 2, rows, 256), BF16),
        vmem((4, 2, rows, 128), BF16),
        vmem((4, rows, 256), BF16),
        vmem((4, 2, 512, 256), BF16),
        vmem((2, 2, 512, 128), BF16),
        vmem((2, 512, 256), BF16),
        vmem((4, 2, 128, 512), BF16),
        vmem((4, 2, 128, 512), BF16),
        vmem((2, 4, 512, 128), BF16),
        vmem((2, 4, 512, 128), BF16),
        vmem((2, 8, 512), I32),
        vmem((5, 4, 512, 512), F32),
        vmem((2, 2, 128, 512), F32),
        vmem((2, 4, 1, 512), F32),
        vmem((2, 128, 512), BF16),
        vmem((2, 128, 512), BF16),
        vmem((2, 8, 512), F32),
        vmem((2, 8, 512), F32),
        vmem((2, 2, 8, 512), F32),
        vmem((2, 8, 512), F32),
        vmem((128, 512), F32),
        vmem((2, 4, rows, 128), BF16),
        vmem((4, rows, 256), BF16),
        vmem((4, 2, 512, 256), F32),
        vmem((2, 2, 128, 512), F32),
        vmem((2, 512, 256), BF16),
        vmem((2, 512, 256), BF16),
        vmem((2, 512, 256), BF16),
        vmem((2, 512, 256), BF16),
        vmem((2, 512, 256), BF16),
        vmem((2, 512, 256), BF16),
        vmem((2, 128, 512), BF16),
        vmem((2, 128, 512), BF16),
        vmem((3, 4, rows, 256), BF16),
        vmem((3, 4, rows, 256), BF16),
        vmem((rows + 2 * HALO, model), BF16),
        vmem((rows, model), F32),
        vmem(conv_kernel.shape, F32),
        pltpu.SMEM(lengths.shape, I32),
        dma(8),
    ]
    for count in (4, 8, 8, 8, 8, 8, 4, 8, 7, 8, 14, 12):
        scratch += [dma(count), dma(count)]
    whole = pl.BlockSpec(memory_space=pltpu.VMEM)
    anywhere = pl.BlockSpec(memory_space=pl.ANY)
    out = jax.ShapeDtypeStruct((rows, model), BF16)
    attended, input_grad = pl.pallas_call(
        functools.partial(layer_kernel, lax.axis_size("ctx")),
        out_shape=(out, out),
        in_specs=[anywhere] * 6,
        out_specs=(whole, whole),
        scratch_shapes=scratch,
        compiler_params=pltpu.CompilerParams(
            collective_id=0, has_side_effects=True, vmem_limit_bytes=66_000_000
        ),
    )(tokens, cotangent, w_qkv, w_out, conv_kernel, lengths)
    return pl.pallas_call(
        settle_kernel,
        out_shape=(out, out),
        in_specs=[anywhere] * 2,
        out_specs=(anywhere, anywhere),
        scratch_shapes=[vmem((2, rows, model), BF16), dma(4)],
    )(attended, input_grad)


def solution(mesh):
    placed = (P(("ctx", "head"), None), P(), P(), P(), P(), P(("ctx", "head"), None))
    return jax.shard_map(
        on_device,
        mesh=mesh,
        in_specs=placed,
        out_specs=(P(("ctx", "head"), None), P(("ctx", "head"), None)),
        check_vma=False,
    )
```
